256 devices in a mesh: seq: 64 (over z, x, core), head: 4 (over y).
Axes of the slice: x: 4, y: 4, z: 8, core: 2. Of those that a mesh axis runs over, the one named last changes fastest.
Arguments:
- query_vectors: bfloat16 [32768, 2048], P('seq', 'head'), may hold values from -6 to 6
- key_vectors: bfloat16 [32768, 2048], P('seq', 'head'), may hold values from -6 to 6
- value_vectors: bfloat16 [32768, 4096], P('seq', 'head'), may hold values from -6 to 6
- query_gain: float32 [16, 32768], P('head', 'seq'), may hold values from 0.25 to 1
- level_gain: float32 [16, 21], P('head'), may hold values from 0.25 to 2
- out_weight: bfloat16 [4096, 2304], P('head'), may hold values from -0.09375 to 0.09375
- out_grad: bfloat16 [32768, 2304], P('seq'), may hold values from -6 to 6
Outputs:
- layer_out: bfloat16 [32768, 2304], P(('seq', 'head'))
- grad_queries: bfloat16 [32768, 2048], P('seq', 'head')
- grad_keys: bfloat16 [32768, 2048], P('seq', 'head')
- grad_values: bfloat16 [32768, 4096], P('seq', 'head')
The draws below stay inside these ranges and needn't reach their ends.
All inputs are finite; a program needn't handle non-finite values.
Results may differ from the reference program's by a relative error of at most 0.012.
Values may be sent and summed in bfloat16 or wider, within the bound.
No kernel may reach another device: no remote copies, remote signals or barrier semaphores. Data moves between devices by JAX's collectives and lax.ppermute only.
A program may use at most 128 MiB of HBM per device.

```python
import math
import jax
import jax.numpy as jnp
from jax import lax

D = 2304
HEADS = 16
DK = 128
DV = 256
LEVELS = 21
TOK_DEV = 512
TOKENS = 32768
N_SEQ = 64


def shard_levels(key, extent, shards, low, top_value):
    def one(position, parts):
        draws = jax.random.uniform(jax.random.fold_in(jax.random.fold_in(key, 6), position), (parts,), jnp.float32, low / len(shards), top_value / len(shards))
        return jnp.repeat(jnp.exp(draws), extent[position] // parts).reshape((-1,) + (1,) * (len(extent) - position - 1))

    loudness = one(*shards[0])
    for cut in shards[1:]:
        loudness = loudness * one(*cut)
    return loudness


def gaussian(stream_key, dims, width, reach, cuts=(), kind=jnp.bfloat16):
    drawn = width * jax.random.normal(stream_key, dims, jnp.float32)
    if cuts:
        drawn = drawn * shard_levels(stream_key, dims, cuts, -0.22, 0.18)
    return jnp.clip(drawn, -reach, reach).astype(kind)


def setup_inputs(seed: int = 0) -> dict:
    splits = jax.random.split(jax.random.key(seed), 8)
    query_vectors = gaussian(splits[0], (TOKENS, HEADS * DK), 1.0, 6.0, ((0, 64), (1, 4)))
    key_vectors = gaussian(splits[1], (TOKENS, HEADS * DK), 1.0, 6.0, ((0, 64), (1, 4)))
    value_vectors = gaussian(splits[2], (TOKENS, HEADS * DV), 1.0, 6.0, ((0, 64), (1, 4)))
    query_gain = jnp.clip(jnp.exp(math.log(1.0) - 1.3862944 * jax.random.uniform(splits[3], (HEADS, TOKENS), jnp.float32) ** shard_levels(splits[3], (HEADS, TOKENS), ((0, 4), (1, 64)), -0.2, 0.2)), 0.25, 1.0)
    level_gain = jnp.clip(jnp.exp(math.log(2.0) - 2.0794415 * jax.random.uniform(splits[4], (HEADS, LEVELS), jnp.float32) ** shard_levels(splits[4], (HEADS, LEVELS), ((0, 4),), -0.2, 0.2)), 0.25, 2.0)
    out_weight = gaussian(splits[5], (HEADS * DV, D), (HEADS * DV) ** -0.5, 0.09375, ((0, 4),))
    out_grad = gaussian(splits[6], (TOKENS, D), 1.0, 6.0, ((0, 64),))
    return dict(query_vectors=query_vectors, key_vectors=key_vectors, value_vectors=value_vectors, query_gain=query_gain, level_gain=level_gain, out_weight=out_weight, out_grad=out_grad)


TOP_LEVEL = lax.Precision.HIGHEST


def bit_length(numbers):
    powers = jnp.left_shift(jnp.int32(1), jnp.arange(31, dtype=jnp.int32))
    return jnp.sum((numbers[..., None] >= powers).astype(jnp.int32), axis=-1)


def level_weights_of(level_gain):
    levels = jnp.arange(level_gain.shape[1], dtype=jnp.int32)
    decline = jnp.exp2(-0.5 * (levels - 1).astype(jnp.float32))
    factor = jnp.where(levels == 0, jnp.float32(1.0), decline).astype(jnp.float32)
    return level_gain * factor[None, :]


def local_table(level_weights, block_rows):
    tokens = jnp.arange(block_rows, dtype=jnp.int32)
    pair_level = bit_length(tokens[:, None] ^ tokens[None, :])
    causal = (tokens[None, :] <= tokens[:, None]).astype(jnp.float32)
    weight_table = jnp.zeros((level_weights.shape[0], block_rows, block_rows), jnp.float32)
    for level_index in range(block_rows.bit_length()):
        weight_table = weight_table + jnp.where(pair_level == level_index, level_weights[:, level_index][:, None, None], jnp.float32(0.0))
    return weight_table * causal


def block_terms(query_per_head, key_per_head, value_per_head, gradient_per_head, query_gain, weight_table, earlier_lower_bits, later_lower_bits, attention_scale):
    query_full_width = query_per_head.astype(jnp.float32)
    key_full_width = key_per_head.astype(jnp.float32)
    value_full_width = value_per_head.astype(jnp.float32)
    gradient_full_width = gradient_per_head.astype(jnp.float32)
    earlier_window_state = earlier_lower_bits.astype(jnp.float32)
    later_window_state = later_lower_bits.astype(jnp.float32)
    pair_weight = query_gain[:, :, None] * weight_table
    level_gain_rows = query_gain.T[:, :, None]
    scores = jnp.einsum('thk,shk->hts', query_full_width, key_full_width, precision=TOP_LEVEL) * attention_scale
    near_weights = (pair_weight * scores).astype(jnp.bfloat16)
    nearby_full_width = near_weights.astype(jnp.float32)
    level_mixing = jnp.einsum('amc,caj->maj', nearby_full_width, value_full_width, precision=TOP_LEVEL) + attention_scale * level_gain_rows * jnp.einsum('sxz,xzg->sxg', query_full_width, earlier_window_state, precision=TOP_LEVEL)
    grad_scores = jnp.einsum('thv,shv->hts', gradient_full_width, value_full_width, precision=TOP_LEVEL)
    nearby_gradients = (attention_scale * pair_weight * grad_scores).astype(jnp.bfloat16).astype(jnp.float32)
    query_gradient = jnp.einsum('xuf,fxl->uxl', nearby_gradients, key_full_width, precision=TOP_LEVEL) + attention_scale * level_gain_rows * jnp.einsum('gbf,bzf->gbz', gradient_full_width, earlier_window_state, precision=TOP_LEVEL)
    key_gradient = jnp.einsum('quw,uqg->wqg', nearby_gradients, query_full_width, precision=TOP_LEVEL) + attention_scale * jnp.einsum('xtl,tzl->xtz', value_full_width, later_window_state, precision=TOP_LEVEL)
    value_gradient = jnp.einsum('fpx,pfj->xfj', nearby_full_width, gradient_full_width, precision=TOP_LEVEL) + attention_scale * jnp.einsum('mwg,wgc->mwc', key_full_width, later_window_state, precision=TOP_LEVEL)
    return level_mixing.astype(jnp.bfloat16), query_gradient.astype(jnp.bfloat16), key_gradient.astype(jnp.bfloat16), value_gradient.astype(jnp.bfloat16)


def reference(query_vectors, key_vectors, value_vectors, query_gain, level_gain, out_weight, out_grad):
    block_rows = TOK_DEV
    block_count = N_SEQ
    attention_scale = DK ** -0.5
    level_weights = level_weights_of(level_gain)
    weight_table = local_table(level_weights, block_rows)
    grad_mixture = jnp.dot(out_grad, out_weight.T, preferred_element_type=jnp.float32).astype(jnp.bfloat16)
    query_blocks = query_vectors.reshape(block_count, block_rows, HEADS, DK)
    key_blocks = key_vectors.reshape(block_count, block_rows, HEADS, DK)
    value_blocks = value_vectors.reshape(block_count, block_rows, HEADS, DV)
    grad_blocks = grad_mixture.reshape(block_count, block_rows, HEADS, DV)
    gain_blocks = query_gain.reshape(HEADS, block_count, block_rows).transpose(1, 0, 2)

    def block_states(pieces):
        key_window_part, value_window_part, query_window_part, grad_piece, gain_piece = pieces
        key_running_state = jnp.einsum('wdp,wdg->dpg', key_window_part.astype(jnp.float32), value_window_part.astype(jnp.float32), precision=TOP_LEVEL)
        scaled_by_gain = (grad_piece.astype(jnp.float32) * gain_piece.T[:, :, None]).astype(jnp.bfloat16)
        scaled_by_gain = lax.optimization_barrier(scaled_by_gain)
        query_running_state = jnp.einsum('wdp,wdg->dpg', query_window_part.astype(jnp.float32), scaled_by_gain.astype(jnp.float32), precision=TOP_LEVEL)
        return key_running_state, query_running_state

    key_state_list, query_state_list = lax.map(block_states, (key_blocks, value_blocks, query_blocks, grad_blocks, gain_blocks))
    shift_bits = block_rows.bit_length() - 1
    block_ids = jnp.arange(block_count, dtype=jnp.int32)
    level_ids = jnp.arange(LEVELS, dtype=jnp.int32)

    def block_sums(index):
        row_levels = bit_length(index ^ block_ids) + shift_bits
        picks = (row_levels[:, None] == level_ids[None, :]).astype(jnp.float32)
        layer_weight_set = jnp.dot(picks, level_weights.T, precision=TOP_LEVEL)
        earlier_token_mask = (block_ids < index).astype(jnp.float32)[:, None]
        later_token_mask = (block_ids > index).astype(jnp.float32)[:, None]
        earlier_window_state = jnp.einsum('jw,jwpz->wpz', layer_weight_set * earlier_token_mask, key_state_list, precision=TOP_LEVEL)
        later_window_state = jnp.einsum('jw,jwpz->wpz', layer_weight_set * later_token_mask, query_state_list, precision=TOP_LEVEL)
        return earlier_window_state.astype(jnp.bfloat16), later_window_state.astype(jnp.bfloat16)

    past_states, future_states = lax.map(block_sums, block_ids)
    past_states, future_states = lax.optimization_barrier((past_states, future_states))

    def block_outputs(pieces):
        query_window_part, key_window_part, value_window_part, grad_piece, gain_piece, past_piece, future_piece = pieces
        return block_terms(query_window_part, key_window_part, value_window_part, grad_piece, gain_piece, weight_table, past_piece, future_piece, attention_scale)

    level_mixing, query_gradient, key_gradient, value_gradient = lax.map(block_outputs, (query_blocks, key_blocks, value_blocks, grad_blocks, gain_blocks, past_states, future_states))
    mixture_rows = level_mixing.reshape(TOKENS, HEADS * DV)
    layer_out = jnp.dot(mixture_rows, out_weight, preferred_element_type=jnp.float32).astype(jnp.bfloat16)
    return (layer_out, query_gradient.reshape(TOKENS, HEADS * DK), key_gradient.reshape(TOKENS, HEADS * DK), value_gradient.reshape(TOKENS, HEADS * DV))
```

```python
import functools

import jax
import jax.numpy as jnp
from jax import lax
from jax.experimental import pallas as pl
from jax.experimental.pallas import tpu as pltpu
from jax.sharding import PartitionSpec as P


F32 = jnp.float32
BF16 = jnp.bfloat16
CONTRACT_LAST = (((1,), (1,)), ((), ()))
CONTRACT_FIRST = (((0,), (0,)), ((), ()))
PLAIN = (((1,), (0,)), ((), ()))
TILE = 256
SMALL = 8 * 2**20
LARGE = 24 * 2**20


def dot(left, right, dims=PLAIN):
    return lax.dot_general(left, right, dims, preferred_element_type=F32)


def vmem(shape=None, index_map=None):
    if shape is None:
        return pl.BlockSpec(memory_space=pltpu.VMEM)
    return pl.BlockSpec(shape, index_map)


def hbm():
    return pl.BlockSpec(memory_space=pltpu.HBM)


def in_hbm(*arrays):
    return [pltpu.with_memory_space_constraint(array, pltpu.HBM) for array in arrays]


def column_of(gain_ref, head):
    row = gain_ref[pl.ds(head, 1)]
    return jnp.transpose(jnp.broadcast_to(row, (8, row.shape[1])), (1, 0))[:, :1]


def smem():
    return pl.BlockSpec(memory_space=pltpu.SMEM)


def cost(flops, moved):
    return pl.CostEstimate(flops=int(flops), bytes_accessed=int(moved), transcendentals=0)


def level_weights_of(level_gain):
    levels = jnp.arange(level_gain.shape[1], dtype=jnp.int32)
    decline = jnp.exp2(-0.5 * (levels - 1).astype(F32))
    factor = jnp.where(levels == 0, F32(1.0), decline)
    return level_gain * factor[None, :]


def key_state_kernel(heads, key_hbm, value_hbm, state_hbm, key_ref, value_ref, state, sems):
    dk, dv = key_ref.shape[1] // heads, value_ref.shape[1] // heads
    loads = []
    for h in range(heads):
        narrow, wide = pl.ds(h * dk, dk), pl.ds(h * dv, dv)
        loads.append(
            (
                pltpu.make_async_copy(key_hbm.at[:, narrow], key_ref.at[:, narrow], sems.at[0, h]),
                pltpu.make_async_copy(value_hbm.at[:, wide], value_ref.at[:, wide], sems.at[1, h]),
            )
        )
    for pair in loads:
        for load in pair:
            load.start()
    stores = []
    for h in range(heads):
        for load in loads[h]:
            load.wait()
        own = pl.ds(h * dk, dk)
        key, value = key_ref[:, h * dk : (h + 1) * dk], value_ref[:, h * dv : (h + 1) * dv]
        state[own] = dot(key, value, CONTRACT_FIRST).astype(BF16)
        stores.append(pltpu.make_async_copy(state.at[own], state_hbm.at[own], sems.at[2, h]))
        stores[-1].start()
    for store in stores:
        store.wait()


def key_state(keys, values, heads):
    rows, dk, dv = keys.shape[0], keys.shape[1] // heads, values.shape[1] // heads
    return pl.pallas_call(
        functools.partial(key_state_kernel, heads),
        in_specs=[hbm(), hbm()],
        out_specs=hbm(),
        out_shape=pltpu.HBM((heads * dk, dv), BF16),
        scratch_shapes=[
            pltpu.VMEM(keys.shape, BF16),
            pltpu.VMEM(values.shape, BF16),
            pltpu.VMEM((heads * dk, dv), BF16),
            pltpu.SemaphoreType.DMA((3, heads)),
        ],
        cost_estimate=cost(2 * rows * dk * dv * heads, 2 * rows * (dk + dv) * heads),
        compiler_params=pltpu.CompilerParams(vmem_limit_bytes=SMALL),
        name="key_state",
    )(*in_hbm(keys, values))


def mix_grad_kernel(
    heads, grad_hbm, weight_hbm, query_hbm, gain_ref, dmix_hbm, state_ref,
    dmix, grad, weight, query, sems,
):
    dk, dv = query.shape[1] // heads, weight.shape[0] // heads
    loads = [
        pltpu.make_async_copy(
            weight_hbm.at[pl.ds(h * dv, dv)], weight.at[pl.ds(h * dv, dv)], sems.at[h]
        )
        for h in range(heads)
    ]
    grad_load = pltpu.make_async_copy(grad_hbm, grad, sems.at[heads])
    query_load = pltpu.make_async_copy(query_hbm, query, sems.at[heads + 1])
    grad_load.start()
    loads[0].start()
    query_load.start()
    for load in loads[1:]:
        load.start()
    grad_load.wait()
    stores = []
    for h in range(heads):
        loads[h].wait()
        own = slice(h * dv, (h + 1) * dv)
        piece = dot(grad[...], weight[own], CONTRACT_LAST).astype(BF16)
        dmix[:, own] = piece
        at = pl.ds(h * dv, dv)
        stores.append(
            pltpu.make_async_copy(dmix.at[:, at], dmix_hbm.at[:, at], sems.at[heads + 2 + h])
        )
        stores[-1].start()
        if h == 0:
            query_load.wait()
        gained = (piece.astype(F32) * column_of(gain_ref, h)).astype(BF16)
        rows = slice(h * dk, (h + 1) * dk)
        state_ref[rows] = dot(query[:, rows], gained, CONTRACT_FIRST).astype(BF16)
    for store in stores:
        store.wait()


def mix_grad(out_grad, out_weight, queries, gain, heads):
    rows, width = out_grad.shape
    dv, dk = out_weight.shape[0] // heads, queries.shape[1] // heads
    return pl.pallas_call(
        functools.partial(mix_grad_kernel, heads),
        in_specs=[hbm(), hbm(), hbm(), vmem()],
        out_specs=[hbm(), vmem()],
        out_shape=[
            pltpu.HBM((rows, heads * dv), BF16),
            jax.ShapeDtypeStruct((heads * dk, dv), BF16),
        ],
        scratch_shapes=[
            pltpu.VMEM((rows, heads * dv), BF16),
            pltpu.VMEM(out_grad.shape, BF16),
            pltpu.VMEM(out_weight.shape, BF16),
            pltpu.VMEM(queries.shape, BF16),
            pltpu.SemaphoreType.DMA((2 * heads + 2,)),
        ],
        cost_estimate=cost(2 * rows * dv * heads * (width + dk), 2 * (rows + dv * heads) * width),
        compiler_params=pltpu.CompilerParams(vmem_limit_bytes=LARGE),
        name="mix_grad",
    )(*in_hbm(out_grad, out_weight, queries), gain)


def scan_pieces(earlier, weight_ref, pieces_ref, write):
    count = pieces_ref.shape[0]
    bits = count.bit_length() - 1
    groups = [[pieces_ref[c].astype(F32) for c in range(count)]]
    for _ in range(bits - 1):
        below = groups[-1]
        groups.append([below[2 * g] + below[2 * g + 1] for g in range(len(below) // 2)])
    carried = [None]
    for bit in reversed(range(bits)):
        weight = weight_ref[0, bit]
        spread = []
        for g, carry in enumerate(carried):
            other = groups[bit][2 * g if earlier else 2 * g + 1] * weight
            total = other if carry is None else carry + other
            spread += [carry, total] if earlier else [total, carry]
        carried = spread
    for c, total in enumerate(carried):
        value = jnp.zeros(pieces_ref.shape[1:], F32) if total is None else total
        write(c, value.astype(BF16))


def scan_past_kernel(weight_ref, pieces_ref, query_ref, joined_ref):
    half = pieces_ref.shape[1]

    def write(c, value):
        joined_ref[c, :half] = value
        joined_ref[c, half:] = query_ref[c]

    scan_pieces(True, weight_ref, pieces_ref, write)


def scan_past(pieces, query_states, weights):
    count, part, width = pieces.shape
    return pl.pallas_call(
        scan_past_kernel,
        in_specs=[smem(), vmem(), vmem()],
        out_specs=vmem(),
        out_shape=jax.ShapeDtypeStruct((count, 2 * part, width), BF16),
        cost_estimate=cost(4 * pieces.size, 8 * pieces.size),
        compiler_params=pltpu.CompilerParams(vmem_limit_bytes=SMALL),
        name="scan_past",
    )(weights, pieces, query_states)


def scan_future_kernel(weight_ref, pieces_ref, sums_ref):
    def write(c, value):
        sums_ref[c] = value

    scan_pieces(False, weight_ref, pieces_ref, write)


def scan_future(joined, weights):
    count, part, width = joined.shape
    part = part // 2
    return pl.pallas_call(
        scan_future_kernel,
        grid=(1,),
        in_specs=[smem(), vmem((count, part, width), lambda i: (0, 1, 0))],
        out_specs=vmem((count, part, width), lambda i: (0, 0, 0)),
        out_shape=jax.ShapeDtypeStruct((count, part, width), BF16),
        cost_estimate=cost(2 * joined.size, 2 * joined.size),
        compiler_params=pltpu.CompilerParams(vmem_limit_bytes=SMALL),
        name="scan_future",
    )(weights, joined)


def near_kernel(
    scale, weight_ref, query_ref, key_ref, value_ref, dmix_ref, gain_ref,
    mix_ref, grad_query_ref, grad_key_ref, grad_value_ref,
):
    head = pl.program_id(0)
    rows = query_ref.shape[0]
    tiles = rows // TILE
    low = TILE.bit_length() - 1
    row = lax.broadcasted_iota(jnp.int32, (TILE, TILE), 0)
    column = lax.broadcasted_iota(jnp.int32, (TILE, TILE), 1)
    apart = row ^ column
    gains = column_of(gain_ref, head)
    table = jnp.full((TILE, TILE), weight_ref[head, 0] * scale, F32)
    for level in range(1, low + 1):
        table = jnp.where(apart >= 2 ** (level - 1), weight_ref[head, level] * scale, table)
    table = jnp.where(column <= row, table, F32(0.0))
    grad_keys = [None] * tiles
    grad_values = [None] * tiles
    for i in range(tiles):
        own = slice(i * TILE, (i + 1) * TILE)
        query, dmix, gain = query_ref[own], dmix_ref[own], gains[own]
        mix = grad_query = None
        for j in range(i + 1):
            other = slice(j * TILE, (j + 1) * TILE)
            key, value = key_ref[other], value_ref[other]
            if i == j:
                pair = gain * table
            else:
                pair = gain * (weight_ref[head, low + (i ^ j).bit_length()] * scale)
            near = (pair * dot(query, key, CONTRACT_LAST)).astype(BF16)
            grad = (pair * dot(dmix, value, CONTRACT_LAST)).astype(BF16)
            terms = (
                dot(near, value),
                dot(grad, key),
                dot(grad, query, CONTRACT_FIRST),
                dot(near, dmix, CONTRACT_FIRST),
            )
            mix = terms[0] if mix is None else mix + terms[0]
            grad_query = terms[1] if grad_query is None else grad_query + terms[1]
            grad_keys[j] = terms[2] if grad_keys[j] is None else grad_keys[j] + terms[2]
            grad_values[j] = terms[3] if grad_values[j] is None else grad_values[j] + terms[3]
        mix_ref[own] = mix.astype(BF16)
        grad_query_ref[own] = grad_query.astype(BF16)
    for j in range(tiles):
        own = slice(j * TILE, (j + 1) * TILE)
        grad_key_ref[own] = grad_keys[j].astype(BF16)
        grad_value_ref[own] = grad_values[j].astype(BF16)


def near_terms(queries, keys, values, dmix, gain, level_weights, scale, heads):
    rows, dk, dv = keys.shape[0], keys.shape[1] // heads, values.shape[1] // heads
    narrow = vmem((rows, dk), lambda h: (0, h))
    wide = vmem((rows, dv), lambda h: (0, h))
    thin, thick = (rows, heads * dk), (rows, heads * dv)
    return pl.pallas_call(
        functools.partial(near_kernel, scale),
        grid=(heads,),
        in_specs=[smem(), narrow, narrow, wide, wide, vmem(gain.shape, lambda h: (0, 0))],
        out_specs=[wide, narrow, narrow, wide],
        out_shape=[pltpu.HBM(shape, BF16) for shape in (thick, thin, thin, thick)],
        cost_estimate=cost(1.5 * rows * rows * heads * 3 * (dk + dv), 8 * rows * heads * (dk + dv)),
        compiler_params=pltpu.CompilerParams(vmem_limit_bytes=LARGE),
        name="near_terms",
    )(level_weights, *in_hbm(queries, keys, values, dmix), gain)


def share_kernel(
    scale, heads, count, index_ref, query_hbm, joined_ref, mix_hbm, gain_ref, weight_hbm, *rest
):
    share_refs, (query, mix, weight, mixture, sems) = rest[: 2 * count], rest[2 * count :]
    rows, dk = query.shape[0], query.shape[1] // heads
    dv = joined_ref.shape[2]
    each = rows // count
    some = joined_ref.shape[0] // heads
    half = weight.shape[1] // 2
    query_load = pltpu.make_async_copy(query_hbm, query, sems.at[0])
    mix_load = pltpu.make_async_copy(mix_hbm, mix, sems.at[1])
    sides = [
        pltpu.make_async_copy(
            weight_hbm.at[:, pl.ds(side * half, half)],
            weight.at[:, pl.ds(side * half, half)],
            sems.at[2 + side],
        )
        for side in range(2)
    ]
    for load in (query_load, mix_load, *sides):
        load.start()
    query_load.wait()
    mix_load.wait()
    for h in range(heads):
        past = joined_ref[h * some : (h + 1) * some, : dk // some].reshape(dk, dv)
        far = dot(query[:, h * dk : (h + 1) * dk], past)
        own = slice(h * dv, (h + 1) * dv)
        piece = (mix[:, own].astype(F32) + (column_of(gain_ref, h) * scale) * far).astype(BF16)
        for c in range(count):
            place = lax.rem(c + count - index_ref[0], count)
            at = pl.ds(pl.multiple_of(place * each, each), each)
            mixture[at, own] = piece[c * each : (c + 1) * each]
    for side in range(2):
        sides[side].wait()
        share = dot(mixture[...], weight[:, side * half : (side + 1) * half]).astype(BF16)
        for step in range(count):
            share_refs[side * count + step][...] = share[step * each : (step + 1) * each]


def shares_of(index, queries, joined, mix, gain, weight, scale, heads, count):
    rows, dk = queries.shape[0], queries.shape[1] // heads
    dv, half = joined.shape[2], weight.shape[1] // 2
    share = jax.ShapeDtypeStruct((rows // count, half), BF16)
    queries, mix, weight = in_hbm(queries, mix, weight)
    shares = pl.pallas_call(
        functools.partial(share_kernel, scale, heads, count),
        in_specs=[smem(), hbm(), vmem(), hbm(), vmem(), hbm()],
        out_specs=[vmem()] * (2 * count),
        out_shape=[share] * (2 * count),
        scratch_shapes=[
            pltpu.VMEM(queries.shape, BF16),
            pltpu.VMEM(mix.shape, BF16),
            pltpu.VMEM(weight.shape, BF16),
            pltpu.VMEM(mix.shape, BF16),
            pltpu.SemaphoreType.DMA((4,)),
        ],
        cost_estimate=cost(2 * rows * dv * heads * (dk + 2 * half), 4 * half * (rows + heads * dv)),
        compiler_params=pltpu.CompilerParams(vmem_limit_bytes=LARGE),
        name="shares",
    )(index, queries, joined, mix, gain, weight)
    return shares[:count], shares[count:]


def add_kernel(left_ref, right_ref, out_ref):
    out_ref[...] = (left_ref[...].astype(F32) + right_ref[...].astype(F32)).astype(BF16)


def added(left, right):
    return pl.pallas_call(
        add_kernel,
        in_specs=[vmem()] * 2,
        out_specs=vmem(),
        out_shape=jax.ShapeDtypeStruct(left.shape, BF16),
        cost_estimate=cost(left.size, 6 * left.size),
        compiler_params=pltpu.CompilerParams(vmem_limit_bytes=SMALL),
        name="added",
    )(left, right)


def total_kernel(*refs):
    *parts, out_ref = refs
    half = parts[0].shape[1]
    for side in range(2):
        a, b, c = (ref[...].astype(F32) for ref in parts[3 * side : 3 * side + 3])
        out_ref[:, side * half : (side + 1) * half] = (a + b + c).astype(BF16)


def total(*parts):
    rows, half = parts[0].shape
    return pl.pallas_call(
        total_kernel,
        in_specs=[vmem()] * 6,
        out_specs=vmem(),
        out_shape=jax.ShapeDtypeStruct((rows, 2 * half), BF16),
        cost_estimate=cost(4 * rows * half, 16 * rows * half),
        compiler_params=pltpu.CompilerParams(vmem_limit_bytes=SMALL),
        name="total",
    )(*parts)


def far_past_kernel(scale, dmix_ref, gain_ref, past_ref, near_ref, grad_ref):
    past = past_ref[...].reshape(near_ref.shape[1], -1)
    far = dot(dmix_ref[...], past, CONTRACT_LAST)
    gain = column_of(gain_ref, pl.program_id(0))
    grad_ref[...] = (near_ref[...].astype(F32) + (gain * scale) * far).astype(BF16)


def far_past(dmix, gain, joined, near, scale, heads):
    rows, dk, dv = near.shape[0], near.shape[1] // heads, dmix.shape[1] // heads
    narrow = vmem((rows, dk), lambda h: (0, h))
    state = vmem((joined.shape[0] // heads, joined.shape[1] // 2, dv), lambda h: (h, 0, 0))
    dmix, near = in_hbm(dmix, near)
    return pl.pallas_call(
        functools.partial(far_past_kernel, scale),
        grid=(heads,),
        in_specs=[
            vmem((rows, dv), lambda h: (0, h)), vmem(gain.shape, lambda h: (0, 0)), state, narrow,
        ],
        out_specs=narrow,
        out_shape=pltpu.HBM(near.shape, BF16),
        cost_estimate=cost(2 * rows * dk * dv * heads, 2 * rows * heads * (2 * dk + dv)),
        compiler_params=pltpu.CompilerParams(vmem_limit_bytes=SMALL),
        name="far_past",
    )(dmix, gain, joined, near)


def far_future_kernel(
    scale, heads, key_hbm, value_hbm, future_ref, near_key_hbm, near_value_hbm,
    grad_key_hbm, grad_value_hbm, key, value, near_key, near_value, grad_key, grad_value, sems,
):
    dk, dv = key.shape[1] // heads, value.shape[1] // heads
    some = future_ref.shape[0] // heads
    loads, stores = [], []
    for h in range(heads):
        thin, thick = pl.ds(h * dk, dk), pl.ds(h * dv, dv)
        for n, (source, target, at) in enumerate(
            (
                (value_hbm, value, thick),
                (near_key_hbm, near_key, thin),
                (key_hbm, key, thin),
                (near_value_hbm, near_value, thick),
            )
        ):
            loads.append(pltpu.make_async_copy(source.at[:, at], target.at[:, at], sems.at[n, h]))
    for load in loads:
        load.start()
    for h in range(heads):
        thin, thick = pl.ds(h * dk, dk), pl.ds(h * dv, dv)
        narrow, wide = slice(h * dk, (h + 1) * dk), slice(h * dv, (h + 1) * dv)
        future = future_ref[h * some : (h + 1) * some].reshape(dk, dv)
        for load in loads[4 * h : 4 * h + 2]:
            load.wait()
        far_key = dot(value[:, wide], future, CONTRACT_LAST)
        grad_key[:, narrow] = (near_key[:, narrow].astype(F32) + scale * far_key).astype(BF16)
        stores.append(
            pltpu.make_async_copy(grad_key.at[:, thin], grad_key_hbm.at[:, thin], sems.at[4, h])
        )
        stores[-1].start()
        for load in loads[4 * h + 2 : 4 * h + 4]:
            load.wait()
        far_value = dot(key[:, narrow], future)
        grad_value[:, wide] = (near_value[:, wide].astype(F32) + scale * far_value).astype(BF16)
        stores.append(
            pltpu.make_async_copy(grad_value.at[:, thick], grad_value_hbm.at[:, thick], sems.at[5, h])
        )
        stores[-1].start()
    for store in stores:
        store.wait()


def far_future(keys, values, future, near_keys, near_values, scale, heads):
    rows, dk, dv = keys.shape[0], keys.shape[1] // heads, values.shape[1] // heads
    thin, thick = keys.shape, values.shape
    keys, values, near_keys, near_values = in_hbm(keys, values, near_keys, near_values)
    return pl.pallas_call(
        functools.partial(far_future_kernel, scale, heads),
        in_specs=[hbm(), hbm(), vmem(), hbm(), hbm()],
        out_specs=[hbm()] * 2,
        out_shape=[pltpu.HBM(thin, BF16), pltpu.HBM(thick, BF16)],
        scratch_shapes=[
            pltpu.VMEM(shape, BF16) for shape in (thin, thick, thin, thick, thin, thick)
        ]
        + [pltpu.SemaphoreType.DMA((6, heads))],
        cost_estimate=cost(4 * rows * dk * dv * heads, 6 * rows * heads * (dk + dv)),
        compiler_params=pltpu.CompilerParams(vmem_limit_bytes=LARGE),
        name="far_future",
    )(keys, values, future, near_keys, near_values)


def in_pieces(states, axis):
    count = lax.axis_size(axis)
    return states.reshape(count, states.shape[0] // count, states.shape[1])


def swapped(pieces, axis):
    return lax.all_to_all(pieces, axis, split_axis=0, concat_axis=0, tiled=True)


def turned(value, axis, step):
    count = lax.axis_size(axis)
    return lax.ppermute(value, axis, [(i, (i + step) % count) for i in range(count)])


def summed_shares(left, right, axis):
    left_far = turned(left[2], axis, 1)
    right_far = turned(right[2], axis, -1)
    right_on = turned(right[1], axis, 1)
    left_back = turned(left[3], axis, -1)
    left_on = turned(added(left[1], left_far), axis, 1)
    right_back = turned(added(right[3], right_far), axis, -1)
    return total(left[0], left_on, left_back, right[0], right_on, right_back)


def on_device(
    query_vectors, key_vectors, value_vectors, query_gain, level_gain, out_weight, out_grad
):
    heads, rows = query_gain.shape
    dk = query_vectors.shape[1] // heads
    scale = dk ** (-0.5)
    seq_count = lax.axis_size("seq")
    bits = seq_count.bit_length() - 1
    shift_bits = rows.bit_length() - 1
    level_weights = level_weights_of(level_gain)
    gain = query_gain
    head = lax.axis_index("seq") // (seq_count // heads)
    scan_weights = lax.dynamic_slice(level_weights, (head, shift_bits + 1), (1, bits))

    key_states = key_state(key_vectors, value_vectors, heads)
    key_pieces = swapped(in_pieces(key_states, "seq"), "seq")
    dmix, query_states = mix_grad(out_grad, out_weight, query_vectors, gain, heads)
    past_pieces = scan_past(key_pieces, in_pieces(query_states, "seq"), scan_weights)
    joined = swapped(past_pieces, "seq")
    mix, near_queries, near_keys, near_values = near_terms(
        query_vectors, key_vectors, value_vectors, dmix, gain, level_weights, scale, heads
    )
    index = lax.axis_index("head").reshape(1)
    left, right = shares_of(
        index, query_vectors, joined, mix, gain, out_weight, scale, heads,
        lax.axis_size("head"),
    )
    layer_out = summed_shares(left, right, "head")
    grad_queries = far_past(dmix, gain, joined, near_queries, scale, heads)
    future_pieces = scan_future(joined, scan_weights)
    future = swapped(future_pieces, "seq")
    grad_keys, grad_values = far_future(
        key_vectors, value_vectors, future, near_keys, near_values, scale, heads
    )
    return (layer_out, grad_queries, grad_keys, grad_values)


def solution(mesh):
    return jax.shard_map(
        on_device,
        mesh=mesh,
        in_specs=(
            P("seq", "head"),
            P("seq", "head"),
            P("seq", "head"),
            P("head", "seq"),
            P("head", None),
            P("head", None),
            P("seq", None),
        ),
        out_specs=(P(("seq", "head"), None), P("seq", "head"), P("seq", "head"), P("seq", "head")),
        check_vma=False,
    )
```

```python
import functools

import jax
import jax.numpy as jnp
from jax import lax
from jax.experimental import pallas as pl
from jax.experimental.pallas import tpu as pltpu
from jax.sharding import PartitionSpec as P


F32 = jnp.float32
BF16 = jnp.bfloat16
CONTRACT_LAST = (((1,), (1,)), ((), ()))
CONTRACT_FIRST = (((0,), (0,)), ((), ()))
PLAIN = (((1,), (0,)), ((), ()))
TILE = 256
SMALL = 8 * 2**20
LARGE = 24 * 2**20


def dot(left, right, dims=PLAIN):
    return lax.dot_general(left, right, dims, preferred_element_type=F32)


def vmem(shape=None, index_map=None):
    if shape is None:
        return pl.BlockSpec(memory_space=pltpu.VMEM)
    return pl.BlockSpec(shape, index_map)


def hbm():
    return pl.BlockSpec(memory_space=pltpu.HBM)


def in_hbm(*arrays):
    return [pltpu.with_memory_space_constraint(array, pltpu.HBM) for array in arrays]


def column_of(gain_ref, head):
    row = gain_ref[pl.ds(head, 1)]
    return jnp.transpose(jnp.broadcast_to(row, (8, row.shape[1])), (1, 0))[:, :1]


def smem():
    return pl.BlockSpec(memory_space=pltpu.SMEM)


def cost(flops, moved):
    return pl.CostEstimate(flops=int(flops), bytes_accessed=int(moved), transcendentals=0)


def level_weights_of(level_gain):
    levels = jnp.arange(level_gain.shape[1], dtype=jnp.int32)
    decline = jnp.exp2(-0.5 * (levels - 1).astype(F32))
    factor = jnp.where(levels == 0, F32(1.0), decline)
    return level_gain * factor[None, :]


def key_state_kernel(heads, key_hbm, value_hbm, state_hbm, key_ref, value_ref, state, sems):
    dk, dv = key_ref.shape[1] // heads, value_ref.shape[1] // heads
    loads = []
    for h in range(heads):
        narrow, wide = pl.ds(h * dk, dk), pl.ds(h * dv, dv)
        loads.append(
            (
                pltpu.make_async_copy(key_hbm.at[:, narrow], key_ref.at[:, narrow], sems.at[0, h]),
                pltpu.make_async_copy(value_hbm.at[:, wide], value_ref.at[:, wide], sems.at[1, h]),
            )
        )
    for pair in loads:
        for load in pair:
            load.start()
    stores = []
    for h in range(heads):
        for load in loads[h]:
            load.wait()
        own = pl.ds(h * dk, dk)
        key, value = key_ref[:, h * dk : (h + 1) * dk], value_ref[:, h * dv : (h + 1) * dv]
        state[own] = dot(key, value, CONTRACT_FIRST).astype(BF16)
        stores.append(pltpu.make_async_copy(state.at[own], state_hbm.at[own], sems.at[2, h]))
        stores[-1].start()
    for store in stores:
        store.wait()


def key_state(keys, values, heads):
    rows, dk, dv = keys.shape[0], keys.shape[1] // heads, values.shape[1] // heads
    return pl.pallas_call(
        functools.partial(key_state_kernel, heads),
        in_specs=[hbm(), hbm()],
        out_specs=hbm(),
        out_shape=pltpu.HBM((heads * dk, dv), BF16),
        scratch_shapes=[
            pltpu.VMEM(keys.shape, BF16),
            pltpu.VMEM(values.shape, BF16),
            pltpu.VMEM((heads * dk, dv), BF16),
            pltpu.SemaphoreType.DMA((3, heads)),
        ],
        cost_estimate=cost(2 * rows * dk * dv * heads, 2 * rows * (dk + dv) * heads),
        compiler_params=pltpu.CompilerParams(vmem_limit_bytes=SMALL),
        name="key_state",
    )(*in_hbm(keys, values))


def mix_grad_kernel(
    heads, grad_hbm, weight_hbm, query_hbm, gain_ref, dmix_hbm, state_ref,
    dmix, grad, weight, query, sems,
):
    dk, dv = query.shape[1] // heads, weight.shape[0] // heads
    pair = 2 * dv

    def started(number, source, target):
        copy = pltpu.make_async_copy(source, target, sems.at[number])
        copy.start()
        return copy

    grad_load = started(0, grad_hbm, grad)
    loads = [
        started(1 + n, weight_hbm.at[pl.ds(n * pair, pair)], weight.at[pl.ds(n * pair, pair)])
        for n in range(heads // 2)
    ]
    query_load = started(1 + heads, query_hbm, query)
    grad_load.wait()
    stores = []
    for n in range(heads // 2):
        loads[n].wait()
        both = slice(n * pair, (n + 1) * pair)
        piece = dot(grad[...], weight[both], CONTRACT_LAST).astype(BF16)
        dmix[:, both] = piece
        at = pl.ds(n * pair, pair)
        stores.append(started(2 + heads + n, dmix.at[:, at], dmix_hbm.at[:, at]))
        if n == 0:
            query_load.wait()
        for h in (2 * n, 2 * n + 1):
            own = piece[:, (h - 2 * n) * dv : (h - 2 * n + 1) * dv].astype(F32)
            gained = (own * column_of(gain_ref, h)).astype(BF16)
            rows = slice(h * dk, (h + 1) * dk)
            state_ref[rows] = dot(query[:, rows], gained, CONTRACT_FIRST).astype(BF16)
    for store in stores:
        store.wait()


def mix_grad(out_grad, out_weight, queries, gain, heads):
    rows, width = out_grad.shape
    dv, dk = out_weight.shape[0] // heads, queries.shape[1] // heads
    return pl.pallas_call(
        functools.partial(mix_grad_kernel, heads),
        in_specs=[hbm(), hbm(), hbm(), vmem()],
        out_specs=[hbm(), vmem()],
        out_shape=[
            pltpu.HBM((rows, heads * dv), BF16),
            jax.ShapeDtypeStruct((heads * dk, dv), BF16),
        ],
        scratch_shapes=[
            pltpu.VMEM((rows, heads * dv), BF16),
            pltpu.VMEM(out_grad.shape, BF16),
            pltpu.VMEM(out_weight.shape, BF16),
            pltpu.VMEM(queries.shape, BF16),
            pltpu.SemaphoreType.DMA((2 * heads + 2,)),
        ],
        cost_estimate=cost(2 * rows * dv * heads * (width + dk), 2 * (rows + dv * heads) * width),
        compiler_params=pltpu.CompilerParams(vmem_limit_bytes=LARGE),
        name="mix_grad",
    )(*in_hbm(out_grad, out_weight, queries), gain)


def scan_pieces(earlier, weight_ref, pieces_ref, write):
    count = pieces_ref.shape[0]
    bits = count.bit_length() - 1
    groups = [[pieces_ref[c].astype(F32) for c in range(count)]]
    for _ in range(bits - 1):
        below = groups[-1]
        groups.append([below[2 * g] + below[2 * g + 1] for g in range(len(below) // 2)])
    carried = [None]
    for bit in reversed(range(bits)):
        weight = weight_ref[0, bit]
        spread = []
        for g, carry in enumerate(carried):
            other = groups[bit][2 * g if earlier else 2 * g + 1] * weight
            total = other if carry is None else carry + other
            spread += [carry, total] if earlier else [total, carry]
        carried = spread
    for c, total in enumerate(carried):
        value = jnp.zeros(pieces_ref.shape[1:], F32) if total is None else total
        write(c, value.astype(BF16))


def scan_past_kernel(weight_ref, pieces_ref, query_ref, joined_ref):
    half = pieces_ref.shape[1]

    def write(c, value):
        joined_ref[c, :half] = value
        joined_ref[c, half:] = query_ref[c]

    scan_pieces(True, weight_ref, pieces_ref, write)


def scan_past(pieces, query_states, weights):
    count, part, width = pieces.shape
    return pl.pallas_call(
        scan_past_kernel,
        in_specs=[smem(), vmem(), vmem()],
        out_specs=vmem(),
        out_shape=jax.ShapeDtypeStruct((count, 2 * part, width), BF16),
        cost_estimate=cost(4 * pieces.size, 8 * pieces.size),
        compiler_params=pltpu.CompilerParams(vmem_limit_bytes=SMALL),
        name="scan_past",
    )(weights, pieces, query_states)


def scan_future_kernel(weight_ref, pieces_ref, sums_ref):
    def write(c, value):
        sums_ref[c] = value

    scan_pieces(False, weight_ref, pieces_ref, write)


def scan_future(joined, weights):
    count, part, width = joined.shape
    part = part // 2
    return pl.pallas_call(
        scan_future_kernel,
        grid=(1,),
        in_specs=[smem(), vmem((count, part, width), lambda i: (0, 1, 0))],
        out_specs=vmem((count, part, width), lambda i: (0, 0, 0)),
        out_shape=jax.ShapeDtypeStruct((count, part, width), BF16),
        cost_estimate=cost(2 * joined.size, 2 * joined.size),
        compiler_params=pltpu.CompilerParams(vmem_limit_bytes=SMALL),
        name="scan_future",
    )(weights, joined)


def near_kernel(
    scale, weight_ref, query_ref, key_ref, value_ref, dmix_ref, gain_ref,
    mix_ref, grad_query_ref, grad_key_ref, grad_value_ref,
):
    head = pl.program_id(0)
    rows = query_ref.shape[0]
    tiles = rows // TILE
    low = TILE.bit_length() - 1
    row = lax.broadcasted_iota(jnp.int32, (TILE, TILE), 0)
    column = lax.broadcasted_iota(jnp.int32, (TILE, TILE), 1)
    apart = row ^ column
    gains = column_of(gain_ref, head)
    table = jnp.full((TILE, TILE), weight_ref[head, 0] * scale, F32)
    for level in range(1, low + 1):
        table = jnp.where(apart >= 2 ** (level - 1), weight_ref[head, level] * scale, table)
    table = jnp.where(column <= row, table, F32(0.0))
    grad_keys = [None] * tiles
    grad_values = [None] * tiles
    for i in range(tiles):
        own = slice(i * TILE, (i + 1) * TILE)
        query, dmix, gain = query_ref[own], dmix_ref[own], gains[own]
        mix = grad_query = None
        for j in range(i + 1):
            other = slice(j * TILE, (j + 1) * TILE)
            key, value = key_ref[other], value_ref[other]
            if i == j:
                pair = gain * table
            else:
                pair = gain * (weight_ref[head, low + (i ^ j).bit_length()] * scale)
            near = (pair * dot(query, key, CONTRACT_LAST)).astype(BF16)
            grad = (pair * dot(dmix, value, CONTRACT_LAST)).astype(BF16)
            terms = (
                dot(near, value),
                dot(grad, key),
                dot(grad, query, CONTRACT_FIRST),
                dot(near, dmix, CONTRACT_FIRST),
            )
            mix = terms[0] if mix is None else mix + terms[0]
            grad_query = terms[1] if grad_query is None else grad_query + terms[1]
            grad_keys[j] = terms[2] if grad_keys[j] is None else grad_keys[j] + terms[2]
            grad_values[j] = terms[3] if grad_values[j] is None else grad_values[j] + terms[3]
        mix_ref[own] = mix.astype(BF16)
        grad_query_ref[own] = grad_query.astype(BF16)
    for j in range(tiles):
        own = slice(j * TILE, (j + 1) * TILE)
        grad_key_ref[own] = grad_keys[j].astype(BF16)
        grad_value_ref[own] = grad_values[j].astype(BF16)


def near_terms(queries, keys, values, dmix, gain, level_weights, scale, heads):
    rows, dk, dv = keys.shape[0], keys.shape[1] // heads, values.shape[1] // heads
    narrow = vmem((rows, dk), lambda h: (0, h))
    wide = vmem((rows, dv), lambda h: (0, h))
    thin, thick = (rows, heads * dk), (rows, heads * dv)
    return pl.pallas_call(
        functools.partial(near_kernel, scale),
        grid=(heads,),
        in_specs=[smem(), narrow, narrow, wide, wide, vmem(gain.shape, lambda h: (0, 0))],
        out_specs=[wide, narrow, narrow, wide],
        out_shape=[pltpu.HBM(shape, BF16) for shape in (thick, thin, thin, thick)],
        cost_estimate=cost(1.5 * rows * rows * heads * 3 * (dk + dv), 8 * rows * heads * (dk + dv)),
        compiler_params=pltpu.CompilerParams(vmem_limit_bytes=LARGE),
        name="near_terms",
    )(level_weights, *in_hbm(queries, keys, values, dmix), gain)


def share_kernel(
    scale, heads, count, index_ref, query_hbm, joined_ref, mix_hbm, gain_ref, weight_hbm, *rest
):
    share_refs, (query, mix, weight, mixture, sems) = rest[: 2 * count], rest[2 * count :]
    rows, dk = query.shape[0], query.shape[1] // heads
    dv = joined_ref.shape[2]
    each = rows // count
    some = joined_ref.shape[0] // heads
    half = weight.shape[1] // 2
    query_load = pltpu.make_async_copy(query_hbm, query, sems.at[0])
    mix_load = pltpu.make_async_copy(mix_hbm, mix, sems.at[1])
    sides = [
        pltpu.make_async_copy(
            weight_hbm.at[:, pl.ds(side * half, half)],
            weight.at[:, pl.ds(side * half, half)],
            sems.at[2 + side],
        )
        for side in range(2)
    ]
    for load in (query_load, mix_load, *sides):
        load.start()
    query_load.wait()
    mix_load.wait()
    for h in range(heads):
        past = joined_ref[h * some : (h + 1) * some, : dk // some].reshape(dk, dv)
        far = dot(query[:, h * dk : (h + 1) * dk], past)
        own = slice(h * dv, (h + 1) * dv)
        piece = (mix[:, own].astype(F32) + (column_of(gain_ref, h) * scale) * far).astype(BF16)
        for c in range(count):
            place = lax.rem(c + count - index_ref[0], count)
            at = pl.ds(pl.multiple_of(place * each, each), each)
            mixture[at, own] = piece[c * each : (c + 1) * each]
    for side in range(2):
        sides[side].wait()
        share = dot(mixture[...], weight[:, side * half : (side + 1) * half]).astype(BF16)
        for step in range(count):
            share_refs[side * count + step][...] = share[step * each : (step + 1) * each]


def shares_of(index, queries, joined, mix, gain, weight, scale, heads, count):
    rows, dk = queries.shape[0], queries.shape[1] // heads
    dv, half = joined.shape[2], weight.shape[1] // 2
    share = jax.ShapeDtypeStruct((rows // count, half), BF16)
    queries, mix, weight = in_hbm(queries, mix, weight)
    shares = pl.pallas_call(
        functools.partial(share_kernel, scale, heads, count),
        in_specs=[smem(), hbm(), vmem(), hbm(), vmem(), hbm()],
        out_specs=[vmem()] * (2 * count),
        out_shape=[share] * (2 * count),
        scratch_shapes=[
            pltpu.VMEM(queries.shape, BF16),
            pltpu.VMEM(mix.shape, BF16),
            pltpu.VMEM(weight.shape, BF16),
            pltpu.VMEM(mix.shape, BF16),
            pltpu.SemaphoreType.DMA((4,)),
        ],
        cost_estimate=cost(2 * rows * dv * heads * (dk + 2 * half), 4 * half * (rows + heads * dv)),
        compiler_params=pltpu.CompilerParams(vmem_limit_bytes=LARGE),
        name="shares",
    )(index, queries, joined, mix, gain, weight)
    return shares[:count], shares[count:]


def add_kernel(left_ref, right_ref, out_ref):
    out_ref[...] = (left_ref[...].astype(F32) + right_ref[...].astype(F32)).astype(BF16)


def added(left, right):
    return pl.pallas_call(
        add_kernel,
        in_specs=[vmem()] * 2,
        out_specs=vmem(),
        out_shape=jax.ShapeDtypeStruct(left.shape, BF16),
        cost_estimate=cost(left.size, 6 * left.size),
        compiler_params=pltpu.CompilerParams(vmem_limit_bytes=SMALL),
        name="added",
    )(left, right)


def total_kernel(*refs):
    *parts, out_ref = refs
    half = parts[0].shape[1]
    for side in range(2):
        a, b, c = (ref[...].astype(F32) for ref in parts[3 * side : 3 * side + 3])
        out_ref[:, side * half : (side + 1) * half] = (a + b + c).astype(BF16)


def total(*parts):
    rows, half = parts[0].shape
    return pl.pallas_call(
        total_kernel,
        in_specs=[vmem()] * 6,
        out_specs=vmem(),
        out_shape=jax.ShapeDtypeStruct((rows, 2 * half), BF16),
        cost_estimate=cost(4 * rows * half, 16 * rows * half),
        compiler_params=pltpu.CompilerParams(vmem_limit_bytes=SMALL),
        name="total",
    )(*parts)


def far_past_kernel(
    scale, heads, dmix_hbm, gain_ref, joined_ref, near_hbm, grad_hbm, dmix, near, grad, sems
):
    dk, dv = near.shape[1] // heads, dmix.shape[1] // heads
    some = joined_ref.shape[0] // heads
    loads, stores = [], []
    for h in range(heads):
        for n, (source, target, size) in enumerate(((dmix_hbm, dmix, dv), (near_hbm, near, dk))):
            at = pl.ds(h * size, size)
            loads.append(pltpu.make_async_copy(source.at[:, at], target.at[:, at], sems.at[n, h]))
            loads[-1].start()
    for h in range(heads):
        past = joined_ref[h * some : (h + 1) * some, : dk // some].reshape(dk, dv)
        for load in loads[2 * h : 2 * h + 2]:
            load.wait()
        far = dot(dmix[:, h * dv : (h + 1) * dv], past, CONTRACT_LAST)
        own, at = slice(h * dk, (h + 1) * dk), pl.ds(h * dk, dk)
        total = near[:, own].astype(F32) + (column_of(gain_ref, h) * scale) * far
        grad[:, own] = total.astype(BF16)
        stores.append(pltpu.make_async_copy(grad.at[:, at], grad_hbm.at[:, at], sems.at[2, h]))
        stores[-1].start()
    for store in stores:
        store.wait()


def far_past(dmix, gain, joined, near, scale, heads):
    rows, dk, dv = near.shape[0], near.shape[1] // heads, dmix.shape[1] // heads
    dmix, near = in_hbm(dmix, near)
    return pl.pallas_call(
        functools.partial(far_past_kernel, scale, heads),
        in_specs=[hbm(), vmem(), vmem(), hbm()],
        out_specs=hbm(),
        out_shape=pltpu.HBM(near.shape, BF16),
        scratch_shapes=[
            pltpu.VMEM(dmix.shape, BF16),
            pltpu.VMEM(near.shape, BF16),
            pltpu.VMEM(near.shape, BF16),
            pltpu.SemaphoreType.DMA((3, heads)),
        ],
        cost_estimate=cost(2 * rows * dk * dv * heads, 2 * rows * heads * (2 * dk + dv)),
        compiler_params=pltpu.CompilerParams(vmem_limit_bytes=SMALL),
        name="far_past",
    )(dmix, gain, joined, near)


def far_future_kernel(
    scale, heads, key_hbm, value_hbm, future_ref, near_key_hbm, near_value_hbm,
    grad_key_hbm, grad_value_hbm, key, value, near_key, near_value, grad_key, grad_value, sems,
):
    dk, dv = key.shape[1] // heads, value.shape[1] // heads
    some = future_ref.shape[0] // heads
    loads, stores = [], []
    for h in range(heads):
        thin, thick = pl.ds(h * dk, dk), pl.ds(h * dv, dv)
        for n, (source, target, at) in enumerate(
            (
                (value_hbm, value, thick),
                (near_key_hbm, near_key, thin),
                (key_hbm, key, thin),
                (near_value_hbm, near_value, thick),
            )
        ):
            loads.append(pltpu.make_async_copy(source.at[:, at], target.at[:, at], sems.at[n, h]))
    for load in loads:
        load.start()
    for h in range(heads):
        thin, thick = pl.ds(h * dk, dk), pl.ds(h * dv, dv)
        narrow, wide = slice(h * dk, (h + 1) * dk), slice(h * dv, (h + 1) * dv)
        future = future_ref[h * some : (h + 1) * some].reshape(dk, dv)
        for load in loads[4 * h : 4 * h + 2]:
            load.wait()
        far_key = dot(value[:, wide], future, CONTRACT_LAST)
        grad_key[:, narrow] = (near_key[:, narrow].astype(F32) + scale * far_key).astype(BF16)
        stores.append(
            pltpu.make_async_copy(grad_key.at[:, thin], grad_key_hbm.at[:, thin], sems.at[4, h])
        )
        stores[-1].start()
        for load in loads[4 * h + 2 : 4 * h + 4]:
            load.wait()
        far_value = dot(key[:, narrow], future)
        grad_value[:, wide] = (near_value[:, wide].astype(F32) + scale * far_value).astype(BF16)
        stores.append(
            pltpu.make_async_copy(grad_value.at[:, thick], grad_value_hbm.at[:, thick], sems.at[5, h])
        )
        stores[-1].start()
    for store in stores:
        store.wait()


def far_future(keys, values, future, near_keys, near_values, scale, heads):
    rows, dk, dv = keys.shape[0], keys.shape[1] // heads, values.shape[1] // heads
    thin, thick = keys.shape, values.shape
    keys, values, near_keys, near_values = in_hbm(keys, values, near_keys, near_values)
    return pl.pallas_call(
        functools.partial(far_future_kernel, scale, heads),
        in_specs=[hbm(), hbm(), vmem(), hbm(), hbm()],
        out_specs=[hbm()] * 2,
        out_shape=[pltpu.HBM(thin, BF16), pltpu.HBM(thick, BF16)],
        scratch_shapes=[
            pltpu.VMEM(shape, BF16) for shape in (thin, thick, thin, thick, thin, thick)
        ]
        + [pltpu.SemaphoreType.DMA((6, heads))],
        cost_estimate=cost(4 * rows * dk * dv * heads, 6 * rows * heads * (dk + dv)),
        compiler_params=pltpu.CompilerParams(vmem_limit_bytes=LARGE),
        name="far_future",
    )(keys, values, future, near_keys, near_values)


def in_pieces(states, axis):
    count = lax.axis_size(axis)
    return states.reshape(count, states.shape[0] // count, states.shape[1])


def swapped(pieces, axis):
    return lax.all_to_all(pieces, axis, split_axis=0, concat_axis=0, tiled=True)


def turned(value, axis, step):
    count = lax.axis_size(axis)
    return lax.ppermute(value, axis, [(i, (i + step) % count) for i in range(count)])


def summed_shares(left, right, axis):
    left_far = turned(left[2], axis, 1)
    right_far = turned(right[2], axis, -1)
    left_back = turned(left[3], axis, -1)
    right_on = turned(right[1], axis, 1)
    left_on = turned(added(left[1], left_far), axis, 1)
    right_back = turned(added(right[3], right_far), axis, -1)
    return total(left[0], left_on, left_back, right[0], right_on, right_back)


def on_device(
    query_vectors, key_vectors, value_vectors, query_gain, level_gain, out_weight, out_grad
):
    heads, rows = query_gain.shape
    dk = query_vectors.shape[1] // heads
    scale = dk ** (-0.5)
    seq_count = lax.axis_size("seq")
    bits = seq_count.bit_length() - 1
    shift_bits = rows.bit_length() - 1
    level_weights = level_weights_of(level_gain)
    gain = query_gain
    head = lax.axis_index("seq") // (seq_count // heads)
    scan_weights = lax.dynamic_slice(level_weights, (head, shift_bits + 1), (1, bits))

    key_states = key_state(key_vectors, value_vectors, heads)
    key_pieces = swapped(in_pieces(key_states, "seq"), "seq")
    dmix, query_states = mix_grad(out_grad, out_weight, query_vectors, gain, heads)
    past_pieces = scan_past(key_pieces, in_pieces(query_states, "seq"), scan_weights)
    joined = swapped(past_pieces, "seq")
    mix, near_queries, near_keys, near_values = near_terms(
        query_vectors, key_vectors, value_vectors, dmix, gain, level_weights, scale, heads
    )
    index = lax.axis_index("head").reshape(1)
    head_count = lax.axis_size("head")
    left, right = shares_of(
        index, query_vectors, joined, mix, gain, out_weight, scale, heads, head_count
    )
    layer_out = summed_shares(left, right, "head")
    grad_queries = far_past(dmix, gain, joined, near_queries, scale, heads)
    future_pieces = scan_future(joined, scan_weights)
    future = swapped(future_pieces, "seq")
    grad_keys, grad_values = far_future(
        key_vectors, value_vectors, future, near_keys, near_values, scale, heads
    )
    return (layer_out, grad_queries, grad_keys, grad_values)


def solution(mesh):
    return jax.shard_map(
        on_device,
        mesh=mesh,
        in_specs=(
            P("seq", "head"),
            P("seq", "head"),
            P("seq", "head"),
            P("head", "seq"),
            P("head", None),
            P("head", None),
            P("seq", None),
        ),
        out_specs=(P(("seq", "head"), None), P("seq", "head"), P("seq", "head"), P("seq", "head")),
        check_vma=False,
    )
```

```python
import functools

import jax
import jax.numpy as jnp
from jax import lax
from jax.experimental import pallas as pl
from jax.experimental.pallas import tpu as pltpu
from jax.sharding import PartitionSpec as P


F32 = jnp.float32
BF16 = jnp.bfloat16
CONTRACT_LAST = (((1,), (1,)), ((), ()))
CONTRACT_FIRST = (((0,), (0,)), ((), ()))
PLAIN = (((1,), (0,)), ((), ()))
TILE = 256
STEP_HEADS = 2
SMALL = 8 * 2**20
LARGE = 24 * 2**20


def dot(left, right, dims=PLAIN):
    return lax.dot_general(left, right, dims, preferred_element_type=F32)


def vmem(shape=None, index_map=None):
    if shape is None:
        return pl.BlockSpec(memory_space=pltpu.VMEM)
    return pl.BlockSpec(shape, index_map)


def hbm():
    return pl.BlockSpec(memory_space=pltpu.HBM)


def in_hbm(*arrays):
    return [pltpu.with_memory_space_constraint(array, pltpu.HBM) for array in arrays]


def column_of(gain_ref, head):
    row = gain_ref[pl.ds(head, 1)]
    return jnp.transpose(jnp.broadcast_to(row, (8, row.shape[1])), (1, 0))[:, :1]


def smem():
    return pl.BlockSpec(memory_space=pltpu.SMEM)


def cost(flops, moved):
    return pl.CostEstimate(flops=int(flops), bytes_accessed=int(moved), transcendentals=0)


def level_weights_of(level_gain):
    levels = jnp.arange(level_gain.shape[1], dtype=jnp.int32)
    decline = jnp.exp2(-0.5 * (levels - 1).astype(F32))
    factor = jnp.where(levels == 0, F32(1.0), decline)
    return level_gain * factor[None, :]


def key_state_kernel(
    heads, core_ref, key_hbm, value_hbm, mine_ref, other_ref, key, value, state, sems
):
    dk, dv = key.shape[1] // heads, value.shape[1] // heads
    loads = []
    for h in range(heads):
        narrow, wide = pl.ds(h * dk, dk), pl.ds(h * dv, dv)
        loads.append(
            (
                pltpu.make_async_copy(key_hbm.at[:, narrow], key.at[:, narrow], sems.at[0, h]),
                pltpu.make_async_copy(value_hbm.at[:, wide], value.at[:, wide], sems.at[1, h]),
            )
        )
    for pair in loads:
        for load in pair:
            load.start()
    for h in range(heads):
        for load in loads[h]:
            load.wait()
        narrow, wide = slice(h * dk, (h + 1) * dk), slice(h * dv, (h + 1) * dv)
        state[narrow] = dot(key[:, narrow], value[:, wide], CONTRACT_FIRST).astype(BF16)
    take_halves(core_ref, state, mine_ref, other_ref)


def take_halves(core_ref, state, mine_ref, other_ref):
    half = mine_ref.shape[0]
    mine_ref[...] = state[pl.ds(pl.multiple_of(core_ref[0] * half, half), half)]
    other_ref[...] = state[pl.ds(pl.multiple_of((1 - core_ref[0]) * half, half), half)]


def key_state(core, keys, values, heads):
    rows, dk, dv = keys.shape[0], keys.shape[1] // heads, values.shape[1] // heads
    return pl.pallas_call(
        functools.partial(key_state_kernel, heads),
        in_specs=[smem(), hbm(), hbm()],
        out_specs=[vmem()] * 2,
        out_shape=[jax.ShapeDtypeStruct((heads * dk // 2, dv), BF16)] * 2,
        scratch_shapes=[
            pltpu.VMEM(keys.shape, BF16),
            pltpu.VMEM(values.shape, BF16),
            pltpu.VMEM((heads * dk, dv), BF16),
            pltpu.SemaphoreType.DMA((2, heads)),
        ],
        cost_estimate=cost(2 * rows * dk * dv * heads, 2 * rows * (dk + dv) * heads),
        compiler_params=pltpu.CompilerParams(vmem_limit_bytes=SMALL),
        name="key_state",
    )(core, *in_hbm(keys, values))


def mix_grad_kernel(
    heads, core_ref, grad_hbm, weight_hbm, query_hbm, gain_ref, dmix_hbm, mine_ref, other_ref,
    dmix, grad, weight, query, state, sems,
):
    dk, dv = query.shape[1] // heads, weight.shape[0] // heads
    pair = 2 * dv

    def started(number, source, target):
        copy = pltpu.make_async_copy(source, target, sems.at[number])
        copy.start()
        return copy

    depth = grad.shape[1] // 3
    firsts = []
    for n in range(3):
        at = pl.ds(n * depth, depth)
        firsts.append(
            (
                started(2 * n, grad_hbm.at[:, at], grad.at[:, at]),
                started(2 * n + 1, weight_hbm.at[pl.ds(0, pair), at], weight.at[pl.ds(0, pair), at]),
            )
        )
    query_load = started(6, query_hbm, query)
    loads = [None] + [
        started(6 + n, weight_hbm.at[pl.ds(n * pair, pair)], weight.at[pl.ds(n * pair, pair)])
        for n in range(1, heads // 2)
    ]
    base = 6 + heads // 2
    stores = []
    for n in range(heads // 2):
        both = slice(n * pair, (n + 1) * pair)
        if n == 0:
            piece = None
            for step, copies in enumerate(firsts):
                for copy in copies:
                    copy.wait()
                at = slice(step * depth, (step + 1) * depth)
                term = dot(grad[:, at], weight[both, at], CONTRACT_LAST)
                piece = term if piece is None else piece + term
        else:
            loads[n].wait()
            piece = dot(grad[...], weight[both], CONTRACT_LAST)
        piece = piece.astype(BF16)
        dmix[:, both] = piece
        at = pl.ds(n * pair, pair)
        stores.append(started(base + n, dmix.at[:, at], dmix_hbm.at[:, at]))
        if n == 0:
            query_load.wait()
        for h in (2 * n, 2 * n + 1):
            own = piece[:, (h - 2 * n) * dv : (h - 2 * n + 1) * dv].astype(F32)
            gained = (own * column_of(gain_ref, h)).astype(BF16)
            rows = slice(h * dk, (h + 1) * dk)
            state[rows] = dot(query[:, rows], gained, CONTRACT_FIRST).astype(BF16)
    take_halves(core_ref, state, mine_ref, other_ref)
    for store in stores:
        store.wait()


def mix_grad(core, out_grad, out_weight, queries, gain, heads):
    rows, width = out_grad.shape
    dv, dk = out_weight.shape[0] // heads, queries.shape[1] // heads
    return pl.pallas_call(
        functools.partial(mix_grad_kernel, heads),
        in_specs=[smem(), hbm(), hbm(), hbm(), vmem()],
        out_specs=[hbm(), vmem(), vmem()],
        out_shape=[
            pltpu.HBM((rows, heads * dv), BF16),
            jax.ShapeDtypeStruct((heads * dk // 2, dv), BF16),
            jax.ShapeDtypeStruct((heads * dk // 2, dv), BF16),
        ],
        scratch_shapes=[
            pltpu.VMEM((rows, heads * dv), BF16),
            pltpu.VMEM(out_grad.shape, BF16),
            pltpu.VMEM(out_weight.shape, BF16),
            pltpu.VMEM(queries.shape, BF16),
            pltpu.VMEM((heads * dk, dv), BF16),
            pltpu.SemaphoreType.DMA((6 + heads,)),
        ],
        cost_estimate=cost(2 * rows * dv * heads * (width + dk), 2 * (rows + dv * heads) * width),
        compiler_params=pltpu.CompilerParams(vmem_limit_bytes=LARGE),
        name="mix_grad",
    )(core, *in_hbm(out_grad, out_weight, queries), gain)


def scan_pieces(earlier, weight_ref, pieces_ref, write):
    count = pieces_ref.shape[0]
    bits = count.bit_length() - 1
    groups = [[pieces_ref[c].astype(F32) for c in range(count)]]
    for _ in range(bits - 1):
        below = groups[-1]
        groups.append([below[2 * g] + below[2 * g + 1] for g in range(len(below) // 2)])
    carried = [None]
    for bit in reversed(range(bits)):
        weight = weight_ref[0, bit]
        spread = []
        for g, carry in enumerate(carried):
            other = groups[bit][2 * g if earlier else 2 * g + 1] * weight
            total = other if carry is None else carry + other
            spread += [carry, total] if earlier else [total, carry]
        carried = spread
    for c, total in enumerate(carried):
        value = jnp.zeros(pieces_ref.shape[1:], F32) if total is None else total
        write(c, value.astype(BF16))


def chip_sum_kernel(mine_ref, other_ref, sum_ref):
    part = sum_ref.shape[1]
    for c in range(sum_ref.shape[0]):
        own = slice(c * part, (c + 1) * part)
        sum_ref[c] = (mine_ref[own].astype(F32) + other_ref[own].astype(F32)).astype(BF16)


def chip_sum(mine, other, count):
    return pl.pallas_call(
        chip_sum_kernel,
        in_specs=[vmem()] * 2,
        out_specs=vmem(),
        out_shape=jax.ShapeDtypeStruct((count, mine.shape[0] // count, mine.shape[1]), BF16),
        cost_estimate=cost(mine.size, 6 * mine.size),
        compiler_params=pltpu.CompilerParams(vmem_limit_bytes=SMALL),
        name="chip_sum",
    )(mine, other)


def scan_past_kernel(weight_ref, pieces_ref, mine_ref, other_ref, joined_ref):
    part = pieces_ref.shape[1]

    def write(c, value):
        own = slice(c * part, (c + 1) * part)
        query = mine_ref[own].astype(F32) + other_ref[own].astype(F32)
        joined_ref[c, :part] = value
        joined_ref[c, part:] = query.astype(BF16)

    scan_pieces(True, weight_ref, pieces_ref, write)


def scan_past(pieces, mine, other, weights):
    count, part, width = pieces.shape
    return pl.pallas_call(
        scan_past_kernel,
        in_specs=[smem()] + [vmem()] * 3,
        out_specs=vmem(),
        out_shape=jax.ShapeDtypeStruct((count, 2 * part, width), BF16),
        cost_estimate=cost(4 * pieces.size, 8 * pieces.size),
        compiler_params=pltpu.CompilerParams(vmem_limit_bytes=SMALL),
        name="scan_past",
    )(weights, pieces, mine, other)


def parts_kernel(earlier, core_ref, weight_ref, shared_ref, mine_ref, other_ref, own_ref, sent_ref):
    part = mine_ref.shape[0] // shared_ref.shape[0]
    heads = weight_ref.shape[0]
    each = mine_ref.shape[0] // heads
    upper = core_ref[0] == 1
    owns = upper if earlier else jnp.logical_not(upper)
    for h in range(heads):
        at = slice(h * each, (h + 1) * each)
        held = slice(h * each // part, (h + 1) * each // part)
        shared = shared_ref[held, :part].reshape(each, -1).astype(F32)
        weight = weight_ref[h, 0]
        with_other = (shared + weight * other_ref[at].astype(F32)).astype(BF16)
        with_mine = (shared + weight * mine_ref[at].astype(F32)).astype(BF16)
        plain = shared.astype(BF16)
        own_ref[at] = jnp.where(owns, with_other, plain)
        sent_ref[at] = jnp.where(owns, plain, with_mine)


def parts_of(core, weights, shared, mine, other, earlier):
    return pl.pallas_call(
        functools.partial(parts_kernel, earlier),
        in_specs=[smem()] * 2 + [vmem()] * 3,
        out_specs=[vmem()] * 2,
        out_shape=[jax.ShapeDtypeStruct(mine.shape, BF16)] * 2,
        cost_estimate=cost(4 * mine.size, 10 * mine.size),
        compiler_params=pltpu.CompilerParams(vmem_limit_bytes=SMALL),
        name="past_parts" if earlier else "future_parts",
    )(core, weights, shared, mine, other)


def state_of(core, own_ref, came_ref, h, heads, dk):
    at = h % (heads // 2)
    own, came = own_ref[at * dk : (at + 1) * dk], came_ref[at * dk : (at + 1) * dk]
    return jnp.where(core == h // (heads // 2), own, came)


def scan_future_kernel(weight_ref, pieces_ref, sums_ref):
    def write(c, value):
        sums_ref[c] = value

    scan_pieces(False, weight_ref, pieces_ref, write)


def scan_future(joined, weights):
    count, part, width = joined.shape
    part = part // 2
    return pl.pallas_call(
        scan_future_kernel,
        grid=(1,),
        in_specs=[smem(), vmem((count, part, width), lambda i: (0, 1, 0))],
        out_specs=vmem((count, part, width), lambda i: (0, 0, 0)),
        out_shape=jax.ShapeDtypeStruct((count, part, width), BF16),
        cost_estimate=cost(2 * joined.size, 2 * joined.size),
        compiler_params=pltpu.CompilerParams(vmem_limit_bytes=SMALL),
        name="scan_future",
    )(weights, joined)


def near_kernel(
    scale, weight_ref, query_ref, key_ref, value_ref, dmix_ref, gain_ref,
    mix_ref, grad_query_ref, grad_key_ref, grad_value_ref,
):
    rows = query_ref.shape[0]
    heads = gain_ref.shape[0] // pl.num_programs(0)
    dk, dv = query_ref.shape[1] // heads, value_ref.shape[1] // heads
    tiles = rows // TILE
    low = TILE.bit_length() - 1
    row = lax.broadcasted_iota(jnp.int32, (TILE, TILE), 0)
    column = lax.broadcasted_iota(jnp.int32, (TILE, TILE), 1)
    apart = row ^ column
    mixes, grad_queries, grad_keys, grad_values = {}, {}, {}, {}

    def add(sums, at, term):
        sums[at] = sums[at] + term if at in sums else term

    each = range(heads)
    names = [pl.program_id(0) * heads + h for h in each]
    gains = [column_of(gain_ref, names[h]) for h in each]
    tables = []
    for h in each:
        table = jnp.full((TILE, TILE), weight_ref[names[h], 0] * scale, F32)
        for level in range(1, low + 1):
            table = jnp.where(
                apart >= 2 ** (level - 1), weight_ref[names[h], level] * scale, table
            )
        tables.append(jnp.where(column <= row, table, F32(0.0)))
    for i in range(tiles):
        own = slice(i * TILE, (i + 1) * TILE)
        for j in range(i + 1):
            other = slice(j * TILE, (j + 1) * TILE)
            thin = [slice(h * dk, (h + 1) * dk) for h in each]
            wide = [slice(h * dv, (h + 1) * dv) for h in each]
            scores = [dot(query_ref[own, thin[h]], key_ref[other, thin[h]], CONTRACT_LAST) for h in each]
            slopes = [dot(dmix_ref[own, wide[h]], value_ref[other, wide[h]], CONTRACT_LAST) for h in each]
            pairs = [
                gains[h][own]
                * (tables[h] if i == j else weight_ref[names[h], low + (i ^ j).bit_length()] * scale)
                for h in each
            ]
            nears = [(pairs[h] * scores[h]).astype(BF16) for h in each]
            grads = [(pairs[h] * slopes[h]).astype(BF16) for h in each]
            for h in each:
                add(mixes, (h, i), dot(nears[h], value_ref[other, wide[h]]))
            for h in each:
                add(grad_queries, (h, i), dot(grads[h], key_ref[other, thin[h]]))
            for h in each:
                add(grad_values, (h, j), dot(nears[h], dmix_ref[own, wide[h]], CONTRACT_FIRST))
            for h in each:
                add(grad_keys, (h, j), dot(grads[h], query_ref[own, thin[h]], CONTRACT_FIRST))
        for h in each:
            mix_ref[own, h * dv : (h + 1) * dv] = mixes[h, i].astype(BF16)
            grad_query_ref[own, h * dk : (h + 1) * dk] = grad_queries[h, i].astype(BF16)
    for j in range(tiles):
        own = slice(j * TILE, (j + 1) * TILE)
        for h in each:
            grad_key_ref[own, h * dk : (h + 1) * dk] = grad_keys[h, j].astype(BF16)
            grad_value_ref[own, h * dv : (h + 1) * dv] = grad_values[h, j].astype(BF16)


def near_terms(queries, keys, values, dmix, gain, level_weights, scale, heads):
    rows, dk, dv = keys.shape[0], keys.shape[1] // heads, values.shape[1] // heads
    narrow = vmem((rows, STEP_HEADS * dk), lambda h: (0, h))
    wide = vmem((rows, STEP_HEADS * dv), lambda h: (0, h))
    thin, thick = (rows, heads * dk), (rows, heads * dv)
    return pl.pallas_call(
        functools.partial(near_kernel, scale),
        grid=(heads // STEP_HEADS,),
        in_specs=[smem(), narrow, narrow, wide, wide, vmem(gain.shape, lambda h: (0, 0))],
        out_specs=[wide, narrow, narrow, wide],
        out_shape=[pltpu.HBM(shape, BF16) for shape in (thick, thin, thin, thick)],
        cost_estimate=cost(1.5 * rows * rows * heads * 3 * (dk + dv), 8 * rows * heads * (dk + dv)),
        compiler_params=pltpu.CompilerParams(vmem_limit_bytes=LARGE),
        name="near_terms",
    )(level_weights, *in_hbm(queries, keys, values, dmix), gain)


def share_kernel(
    scale, heads, count, index_ref, query_hbm, own_ref, came_ref, mix_hbm, gain_ref, weight_hbm, *rest
):
    share_refs, (query, mix, weight, mixture, sems) = rest[: 2 * count], rest[2 * count :]
    rows, dk = query.shape[0], query.shape[1] // heads
    dv = own_ref.shape[1]
    each = rows // count
    half = weight.shape[1] // 2
    query_load = pltpu.make_async_copy(query_hbm, query, sems.at[0])
    mix_load = pltpu.make_async_copy(mix_hbm, mix, sems.at[1])
    sides = [
        pltpu.make_async_copy(
            weight_hbm.at[:, pl.ds(side * half, half)],
            weight.at[:, pl.ds(side * half, half)],
            sems.at[2 + side],
        )
        for side in range(2)
    ]
    for load in (query_load, mix_load, *sides):
        load.start()
    query_load.wait()
    mix_load.wait()
    for h in range(heads):
        past = state_of(index_ref[1], own_ref, came_ref, h, heads, dk)
        far = dot(query[:, h * dk : (h + 1) * dk], past)
        own = slice(h * dv, (h + 1) * dv)
        piece = (mix[:, own].astype(F32) + (column_of(gain_ref, h) * scale) * far).astype(BF16)
        for c in range(count):
            place = lax.rem(c + count - index_ref[0], count)
            at = pl.ds(pl.multiple_of(place * each, each), each)
            mixture[at, own] = piece[c * each : (c + 1) * each]
    for side in range(2):
        sides[side].wait()
        share = dot(mixture[...], weight[:, side * half : (side + 1) * half]).astype(BF16)
        for step in range(count):
            share_refs[side * count + step][...] = share[step * each : (step + 1) * each]


def shares_of(index, queries, own, came, mix, gain, weight, scale, heads, count):
    rows, dk = queries.shape[0], queries.shape[1] // heads
    dv, half = own.shape[1], weight.shape[1] // 2
    share = jax.ShapeDtypeStruct((rows // count, half), BF16)
    queries, mix, weight = in_hbm(queries, mix, weight)
    shares = pl.pallas_call(
        functools.partial(share_kernel, scale, heads, count),
        in_specs=[smem(), hbm(), vmem(), vmem(), hbm(), vmem(), hbm()],
        out_specs=[vmem()] * (2 * count),
        out_shape=[share] * (2 * count),
        scratch_shapes=[
            pltpu.VMEM(queries.shape, BF16),
            pltpu.VMEM(mix.shape, BF16),
            pltpu.VMEM(weight.shape, BF16),
            pltpu.VMEM(mix.shape, BF16),
            pltpu.SemaphoreType.DMA((4,)),
        ],
        cost_estimate=cost(2 * rows * dv * heads * (dk + 2 * half), 4 * half * (rows + heads * dv)),
        compiler_params=pltpu.CompilerParams(vmem_limit_bytes=LARGE),
        name="shares",
    )(index, queries, own, came, mix, gain, weight)
    return shares[:count], shares[count:]


def add_kernel(left_ref, right_ref, out_ref):
    out_ref[...] = (left_ref[...].astype(F32) + right_ref[...].astype(F32)).astype(BF16)


def added(left, right):
    return pl.pallas_call(
        add_kernel,
        in_specs=[vmem()] * 2,
        out_specs=vmem(),
        out_shape=jax.ShapeDtypeStruct(left.shape, BF16),
        cost_estimate=cost(left.size, 6 * left.size),
        compiler_params=pltpu.CompilerParams(vmem_limit_bytes=SMALL),
        name="added",
    )(left, right)


def total_kernel(*refs):
    *parts, out_ref = refs
    half = parts[0].shape[1]
    for side in range(2):
        a, b, c = (ref[...].astype(F32) for ref in parts[3 * side : 3 * side + 3])
        out_ref[:, side * half : (side + 1) * half] = (a + b + c).astype(BF16)


def total(*parts):
    rows, half = parts[0].shape
    return pl.pallas_call(
        total_kernel,
        in_specs=[vmem()] * 6,
        out_specs=vmem(),
        out_shape=jax.ShapeDtypeStruct((rows, 2 * half), BF16),
        cost_estimate=cost(4 * rows * half, 16 * rows * half),
        compiler_params=pltpu.CompilerParams(vmem_limit_bytes=SMALL),
        name="total",
    )(*parts)


def far_past_kernel(
    scale, heads, core_ref, dmix_hbm, gain_ref, own_ref, came_ref, near_hbm, grad_hbm,
    dmix, near, grad, sems,
):
    dk, dv = near.shape[1] // heads, dmix.shape[1] // heads
    loads, stores = [], []
    for h in range(heads):
        for n, (source, target, size) in enumerate(((dmix_hbm, dmix, dv), (near_hbm, near, dk))):
            at = pl.ds(h * size, size)
            loads.append(pltpu.make_async_copy(source.at[:, at], target.at[:, at], sems.at[n, h]))
            loads[-1].start()
    for h in range(heads):
        past = state_of(core_ref[0], own_ref, came_ref, h, heads, dk)
        for load in loads[2 * h : 2 * h + 2]:
            load.wait()
        far = dot(dmix[:, h * dv : (h + 1) * dv], past, CONTRACT_LAST)
        own, at = slice(h * dk, (h + 1) * dk), pl.ds(h * dk, dk)
        total = near[:, own].astype(F32) + (column_of(gain_ref, h) * scale) * far
        grad[:, own] = total.astype(BF16)
        stores.append(pltpu.make_async_copy(grad.at[:, at], grad_hbm.at[:, at], sems.at[2, h]))
        stores[-1].start()
    for store in stores:
        store.wait()


def far_past(core, dmix, gain, own, came, near, scale, heads):
    rows, dk, dv = near.shape[0], near.shape[1] // heads, dmix.shape[1] // heads
    dmix, near = in_hbm(dmix, near)
    return pl.pallas_call(
        functools.partial(far_past_kernel, scale, heads),
        in_specs=[smem(), hbm(), vmem(), vmem(), vmem(), hbm()],
        out_specs=hbm(),
        out_shape=pltpu.HBM(near.shape, BF16),
        scratch_shapes=[
            pltpu.VMEM(dmix.shape, BF16),
            pltpu.VMEM(near.shape, BF16),
            pltpu.VMEM(near.shape, BF16),
            pltpu.SemaphoreType.DMA((3, heads)),
        ],
        cost_estimate=cost(2 * rows * dk * dv * heads, 2 * rows * heads * (2 * dk + dv)),
        compiler_params=pltpu.CompilerParams(vmem_limit_bytes=SMALL),
        name="far_past",
    )(core, dmix, gain, own, came, near)


def far_future_kernel(
    scale, heads, core_ref, key_hbm, value_hbm, own_ref, came_ref, near_key_hbm, near_value_hbm,
    grad_key_hbm, grad_value_hbm, key, value, near_key, near_value, grad_key, grad_value, sems,
):
    dk, dv = key.shape[1] // heads, value.shape[1] // heads
    loads, stores = [], []
    for h in range(heads):
        thin, thick = pl.ds(h * dk, dk), pl.ds(h * dv, dv)
        for n, (source, target, at) in enumerate(
            (
                (value_hbm, value, thick),
                (near_key_hbm, near_key, thin),
                (key_hbm, key, thin),
                (near_value_hbm, near_value, thick),
            )
        ):
            loads.append(pltpu.make_async_copy(source.at[:, at], target.at[:, at], sems.at[n, h]))
    for load in loads:
        load.start()
    for h in range(heads):
        thin, thick = pl.ds(h * dk, dk), pl.ds(h * dv, dv)
        narrow, wide = slice(h * dk, (h + 1) * dk), slice(h * dv, (h + 1) * dv)
        future = state_of(core_ref[0], own_ref, came_ref, h, heads, dk)
        for load in loads[4 * h : 4 * h + 2]:
            load.wait()
        far_key = dot(value[:, wide], future, CONTRACT_LAST)
        grad_key[:, narrow] = (near_key[:, narrow].astype(F32) + scale * far_key).astype(BF16)
        stores.append(
            pltpu.make_async_copy(grad_key.at[:, thin], grad_key_hbm.at[:, thin], sems.at[4, h])
        )
        stores[-1].start()
        for load in loads[4 * h + 2 : 4 * h + 4]:
            load.wait()
        far_value = dot(key[:, narrow], future)
        grad_value[:, wide] = (near_value[:, wide].astype(F32) + scale * far_value).astype(BF16)
        stores.append(
            pltpu.make_async_copy(grad_value.at[:, thick], grad_value_hbm.at[:, thick], sems.at[5, h])
        )
        stores[-1].start()
    for store in stores:
        store.wait()


def far_future(core, keys, values, own, came, near_keys, near_values, scale, heads):
    rows, dk, dv = keys.shape[0], keys.shape[1] // heads, values.shape[1] // heads
    thin, thick = keys.shape, values.shape
    keys, values, near_keys, near_values = in_hbm(keys, values, near_keys, near_values)
    return pl.pallas_call(
        functools.partial(far_future_kernel, scale, heads),
        in_specs=[smem(), hbm(), hbm(), vmem(), vmem(), hbm(), hbm()],
        out_specs=[hbm()] * 2,
        out_shape=[pltpu.HBM(thin, BF16), pltpu.HBM(thick, BF16)],
        scratch_shapes=[
            pltpu.VMEM(shape, BF16) for shape in (thin, thick, thin, thick, thin, thick)
        ]
        + [pltpu.SemaphoreType.DMA((6, heads))],
        cost_estimate=cost(4 * rows * dk * dv * heads, 6 * rows * heads * (dk + dv)),
        compiler_params=pltpu.CompilerParams(vmem_limit_bytes=LARGE),
        name="far_future",
    )(core, keys, values, own, came, near_keys, near_values)


def swapped(pieces, axis, groups):
    return lax.all_to_all(
        pieces, axis, split_axis=0, concat_axis=0, tiled=True, axis_index_groups=groups
    )


def from_sibling(value, axis):
    return lax.ppermute(value, axis, [(i, i ^ 1) for i in range(lax.axis_size(axis))])


def turned(value, axis, step):
    count = lax.axis_size(axis)
    return lax.ppermute(value, axis, [(i, (i + step) % count) for i in range(count)])


def summed_shares(left, right, axis):
    left_far = turned(left[2], axis, 1)
    right_far = turned(right[2], axis, -1)
    left_back = turned(left[3], axis, -1)
    right_on = turned(right[1], axis, 1)
    left_on = turned(added(left[1], left_far), axis, 1)
    right_back = turned(added(right[3], right_far), axis, -1)
    return total(left[0], left_on, left_back, right[0], right_on, right_back)


def on_device(
    query_vectors, key_vectors, value_vectors, query_gain, level_gain, out_weight, out_grad
):
    heads, rows = query_gain.shape
    dk = query_vectors.shape[1] // heads
    scale = dk ** (-0.5)
    seq_count = lax.axis_size("seq")
    bits = seq_count.bit_length() - 1
    shift_bits = rows.bit_length() - 1
    level_weights = level_weights_of(level_gain)
    gain = query_gain
    chips = seq_count // 2
    groups = [[2 * chip + core for chip in range(chips)] for core in range(2)]
    chip, core = lax.axis_index("seq") // 2, lax.axis_index("seq") % 2
    head = core * (heads // 2) + chip * (heads // 2) // chips
    scan_weights = lax.dynamic_slice(level_weights, (head, shift_bits + 2), (1, bits - 1))
    pair_weights = lax.dynamic_slice(
        level_weights, (core * (heads // 2), shift_bits + 1), (heads // 2, 1)
    )
    index = jnp.stack([lax.axis_index("head"), core])
    core = core.reshape(1)

    key_mine, key_sent = key_state(core, key_vectors, value_vectors, heads)
    key_other = from_sibling(key_sent, "seq")
    key_pieces = swapped(chip_sum(key_mine, key_other, chips), "seq", groups)
    dmix, query_mine, query_sent = mix_grad(core, out_grad, out_weight, query_vectors, gain, heads)
    query_other = from_sibling(query_sent, "seq")
    past_pieces = scan_past(key_pieces, query_mine, query_other, scan_weights)
    joined = swapped(past_pieces, "seq", groups)
    mix, near_queries, near_keys, near_values = near_terms(
        query_vectors, key_vectors, value_vectors, dmix, gain, level_weights, scale, heads
    )
    past_own, past_sent = parts_of(core, pair_weights, joined, key_mine, key_other, True)
    past_came = from_sibling(past_sent, "seq")
    left, right = shares_of(
        index, query_vectors, past_own, past_came, mix, gain, out_weight, scale, heads,
        lax.axis_size("head"),
    )
    layer_out = summed_shares(left, right, "head")
    grad_queries = far_past(core, dmix, gain, past_own, past_came, near_queries, scale, heads)
    future_pieces = scan_future(joined, scan_weights)
    future = swapped(future_pieces, "seq", groups)
    future_own, future_sent = parts_of(core, pair_weights, future, query_mine, query_other, False)
    future_came = from_sibling(future_sent, "seq")
    grad_keys, grad_values = far_future(
        core, key_vectors, value_vectors, future_own, future_came, near_keys, near_values,
        scale, heads,
    )
    return (layer_out, grad_queries, grad_keys, grad_values)


def solution(mesh):
    return jax.shard_map(
        on_device,
        mesh=mesh,
        in_specs=(
            P("seq", "head"),
            P("seq", "head"),
            P("seq", "head"),
            P("head", "seq"),
            P("head", None),
            P("head", None),
            P("seq", None),
        ),
        out_specs=(P(("seq", "head"), None), P("seq", "head"), P("seq", "head"), P("seq", "head")),
        check_vma=False,
    )
```

```python
import functools

import jax
import jax.numpy as jnp
from jax import lax
from jax.experimental import pallas as pl
from jax.experimental.pallas import tpu as pltpu
from jax.sharding import PartitionSpec as P


F32 = jnp.float32
BF16 = jnp.bfloat16
CONTRACT_LAST = (((1,), (1,)), ((), ()))
CONTRACT_FIRST = (((0,), (0,)), ((), ()))
PLAIN = (((1,), (0,)), ((), ()))
TILE = 256
STEP_HEADS = 2
SMALL = 8 * 2**20
LARGE = 24 * 2**20


def dot(left, right, dims=PLAIN):
    return lax.dot_general(left, right, dims, preferred_element_type=F32)


def vmem(shape=None, index_map=None):
    if shape is None:
        return pl.BlockSpec(memory_space=pltpu.VMEM)
    return pl.BlockSpec(shape, index_map)


def hbm():
    return pl.BlockSpec(memory_space=pltpu.HBM)


def in_hbm(*arrays):
    return [pltpu.with_memory_space_constraint(array, pltpu.HBM) for array in arrays]


def column_of(gain_ref, head):
    row = gain_ref[pl.ds(head, 1)]
    return jnp.transpose(jnp.broadcast_to(row, (8, row.shape[1])), (1, 0))[:, :1]


def smem():
    return pl.BlockSpec(memory_space=pltpu.SMEM)


def cost(flops, moved):
    return pl.CostEstimate(flops=int(flops), bytes_accessed=int(moved), transcendentals=0)


def level_weights_of(level_gain):
    levels = jnp.arange(level_gain.shape[1], dtype=jnp.int32)
    decline = jnp.exp2(-0.5 * (levels - 1).astype(F32))
    factor = jnp.where(levels == 0, F32(1.0), decline)
    return level_gain * factor[None, :]


def key_state_kernel(
    heads, core_ref, key_hbm, value_hbm, mine_ref, other_ref, key, value, state, sems
):
    dk, dv = key.shape[1] // heads, value.shape[1] // heads
    loads = []
    for h in range(heads):
        narrow, wide = pl.ds(h * dk, dk), pl.ds(h * dv, dv)
        loads.append(
            (
                pltpu.make_async_copy(key_hbm.at[:, narrow], key.at[:, narrow], sems.at[0, h]),
                pltpu.make_async_copy(value_hbm.at[:, wide], value.at[:, wide], sems.at[1, h]),
            )
        )
    for pair in loads:
        for load in pair:
            load.start()
    for h in range(heads):
        for load in loads[h]:
            load.wait()
        narrow, wide = slice(h * dk, (h + 1) * dk), slice(h * dv, (h + 1) * dv)
        state[narrow] = dot(key[:, narrow], value[:, wide], CONTRACT_FIRST).astype(BF16)
    take_halves(core_ref, state, mine_ref, other_ref)


def take_halves(core_ref, state, mine_ref, other_ref):
    half = mine_ref.shape[0]
    mine_ref[...] = state[pl.ds(pl.multiple_of(core_ref[0] * half, half), half)]
    other_ref[...] = state[pl.ds(pl.multiple_of((1 - core_ref[0]) * half, half), half)]


def key_state(core, keys, values, heads):
    rows, dk, dv = keys.shape[0], keys.shape[1] // heads, values.shape[1] // heads
    return pl.pallas_call(
        functools.partial(key_state_kernel, heads),
        in_specs=[smem(), hbm(), hbm()],
        out_specs=[vmem()] * 2,
        out_shape=[jax.ShapeDtypeStruct((heads * dk // 2, dv), BF16)] * 2,
        scratch_shapes=[
            pltpu.VMEM(keys.shape, BF16),
            pltpu.VMEM(values.shape, BF16),
            pltpu.VMEM((heads * dk, dv), BF16),
            pltpu.SemaphoreType.DMA((2, heads)),
        ],
        cost_estimate=cost(2 * rows * dk * dv * heads, 2 * rows * (dk + dv) * heads),
        compiler_params=pltpu.CompilerParams(vmem_limit_bytes=SMALL),
        name="key_state",
    )(core, *in_hbm(keys, values))


def mix_grad_kernel(
    heads, core_ref, grad_hbm, weight_hbm, query_hbm, gain_hbm, dmix_hbm, mine_ref, other_ref,
    dmix, grad, weight, query, state, gain_ref, sems,
):
    dk, dv = query.shape[1] // heads, weight.shape[0] // heads
    pair = 2 * dv

    def started(number, source, target):
        copy = pltpu.make_async_copy(source, target, sems.at[number])
        copy.start()
        return copy

    depth = grad.shape[1] // 3
    firsts = []
    for n in range(3):
        at = pl.ds(n * depth, depth)
        firsts.append(
            (
                started(2 * n, grad_hbm.at[:, at], grad.at[:, at]),
                started(2 * n + 1, weight_hbm.at[pl.ds(0, pair), at], weight.at[pl.ds(0, pair), at]),
            )
        )
    query_load = started(6, query_hbm, query)
    gain_load = started(6 + heads, gain_hbm, gain_ref)
    loads = [None] + [
        started(6 + n, weight_hbm.at[pl.ds(n * pair, pair)], weight.at[pl.ds(n * pair, pair)])
        for n in range(1, heads // 2)
    ]
    base = 6 + heads // 2
    stores = []
    for n in range(heads // 2):
        both = slice(n * pair, (n + 1) * pair)
        if n == 0:
            piece = None
            for step, copies in enumerate(firsts):
                for copy in copies:
                    copy.wait()
                at = slice(step * depth, (step + 1) * depth)
                term = dot(grad[:, at], weight[both, at], CONTRACT_LAST)
                piece = term if piece is None else piece + term
        else:
            loads[n].wait()
            piece = dot(grad[...], weight[both], CONTRACT_LAST)
        piece = piece.astype(BF16)
        dmix[:, both] = piece
        at = pl.ds(n * pair, pair)
        stores.append(started(base + n, dmix.at[:, at], dmix_hbm.at[:, at]))
        if n == 0:
            query_load.wait()
            gain_load.wait()
        for h in (2 * n, 2 * n + 1):
            own = piece[:, (h - 2 * n) * dv : (h - 2 * n + 1) * dv].astype(F32)
            gained = (own * column_of(gain_ref, h)).astype(BF16)
            rows = slice(h * dk, (h + 1) * dk)
            state[rows] = dot(query[:, rows], gained, CONTRACT_FIRST).astype(BF16)
    take_halves(core_ref, state, mine_ref, other_ref)
    for store in stores:
        store.wait()


def mix_grad(core, out_grad, out_weight, queries, gain, heads):
    rows, width = out_grad.shape
    dv, dk = out_weight.shape[0] // heads, queries.shape[1] // heads
    return pl.pallas_call(
        functools.partial(mix_grad_kernel, heads),
        in_specs=[smem(), hbm(), hbm(), hbm(), hbm()],
        out_specs=[hbm(), vmem(), vmem()],
        out_shape=[
            pltpu.HBM((rows, heads * dv), BF16),
            jax.ShapeDtypeStruct((heads * dk // 2, dv), BF16),
            jax.ShapeDtypeStruct((heads * dk // 2, dv), BF16),
        ],
        scratch_shapes=[
            pltpu.VMEM((rows, heads * dv), BF16),
            pltpu.VMEM(out_grad.shape, BF16),
            pltpu.VMEM(out_weight.shape, BF16),
            pltpu.VMEM(queries.shape, BF16),
            pltpu.VMEM((heads * dk, dv), BF16),
            pltpu.VMEM(gain.shape, F32),
            pltpu.SemaphoreType.DMA((7 + heads,)),
        ],
        cost_estimate=cost(2 * rows * dv * heads * (width + dk), 2 * (rows + dv * heads) * width),
        compiler_params=pltpu.CompilerParams(vmem_limit_bytes=LARGE),
        name="mix_grad",
    )(core, *in_hbm(out_grad, out_weight, queries, gain))


def scan_pieces(earlier, weight_ref, pieces_ref, write):
    count = pieces_ref.shape[0]
    bits = count.bit_length() - 1
    groups = [[pieces_ref[c].astype(F32) for c in range(count)]]
    for _ in range(bits - 1):
        below = groups[-1]
        groups.append([below[2 * g] + below[2 * g + 1] for g in range(len(below) // 2)])
    carried = [None]
    for bit in reversed(range(bits)):
        weight = weight_ref[0, bit]
        spread = []
        for g, carry in enumerate(carried):
            other = groups[bit][2 * g if earlier else 2 * g + 1] * weight
            total = other if carry is None else carry + other
            spread += [carry, total] if earlier else [total, carry]
        carried = spread
    for c, total in enumerate(carried):
        value = jnp.zeros(pieces_ref.shape[1:], F32) if total is None else total
        write(c, value.astype(BF16))


def chip_sum_kernel(mine_ref, other_ref, sum_ref):
    part = sum_ref.shape[1]
    for c in range(sum_ref.shape[0]):
        own = slice(c * part, (c + 1) * part)
        sum_ref[c] = (mine_ref[own].astype(F32) + other_ref[own].astype(F32)).astype(BF16)


def chip_sum(mine, other, count):
    return pl.pallas_call(
        chip_sum_kernel,
        in_specs=[vmem()] * 2,
        out_specs=vmem(),
        out_shape=jax.ShapeDtypeStruct((count, mine.shape[0] // count, mine.shape[1]), BF16),
        cost_estimate=cost(mine.size, 6 * mine.size),
        compiler_params=pltpu.CompilerParams(vmem_limit_bytes=SMALL),
        name="chip_sum",
    )(mine, other)


def scan_past_kernel(weight_ref, pieces_ref, mine_ref, other_ref, joined_ref):
    part = pieces_ref.shape[1]

    def write(c, value):
        own = slice(c * part, (c + 1) * part)
        query = mine_ref[own].astype(F32) + other_ref[own].astype(F32)
        joined_ref[c, :part] = value
        joined_ref[c, part:] = query.astype(BF16)

    scan_pieces(True, weight_ref, pieces_ref, write)


def scan_past(pieces, mine, other, weights):
    count, part, width = pieces.shape
    return pl.pallas_call(
        scan_past_kernel,
        in_specs=[smem()] + [vmem()] * 3,
        out_specs=vmem(),
        out_shape=jax.ShapeDtypeStruct((count, 2 * part, width), BF16),
        cost_estimate=cost(4 * pieces.size, 8 * pieces.size),
        compiler_params=pltpu.CompilerParams(vmem_limit_bytes=SMALL),
        name="scan_past",
    )(weights, pieces, mine, other)


def parts_kernel(earlier, core_ref, weight_ref, shared_ref, mine_ref, other_ref, own_ref, sent_ref):
    part = mine_ref.shape[0] // shared_ref.shape[0]
    heads = weight_ref.shape[0]
    each = mine_ref.shape[0] // heads
    upper = core_ref[0] == 1
    owns = upper if earlier else jnp.logical_not(upper)
    for h in range(heads):
        at = slice(h * each, (h + 1) * each)
        held = slice(h * each // part, (h + 1) * each // part)
        shared = shared_ref[held, :part].reshape(each, -1).astype(F32)
        weight = weight_ref[h, 0]
        with_other = (shared + weight * other_ref[at].astype(F32)).astype(BF16)
        with_mine = (shared + weight * mine_ref[at].astype(F32)).astype(BF16)
        plain = shared.astype(BF16)
        own_ref[at] = jnp.where(owns, with_other, plain)
        sent_ref[at] = jnp.where(owns, plain, with_mine)


def parts_of(core, weights, shared, mine, other, earlier):
    return pl.pallas_call(
        functools.partial(parts_kernel, earlier),
        in_specs=[smem()] * 2 + [vmem()] * 3,
        out_specs=[vmem()] * 2,
        out_shape=[jax.ShapeDtypeStruct(mine.shape, BF16)] * 2,
        cost_estimate=cost(4 * mine.size, 10 * mine.size),
        compiler_params=pltpu.CompilerParams(vmem_limit_bytes=SMALL),
        name="past_parts" if earlier else "future_parts",
    )(core, weights, shared, mine, other)


def state_of(core, own_ref, came_ref, h, heads, dk):
    at = h % (heads // 2)
    own, came = own_ref[at * dk : (at + 1) * dk], came_ref[at * dk : (at + 1) * dk]
    return jnp.where(core == h // (heads // 2), own, came)


def scan_future_kernel(weight_ref, pieces_ref, sums_ref):
    def write(c, value):
        sums_ref[c] = value

    scan_pieces(False, weight_ref, pieces_ref, write)


def scan_future(joined, weights):
    count, part, width = joined.shape
    part = part // 2
    return pl.pallas_call(
        scan_future_kernel,
        grid=(1,),
        in_specs=[smem(), vmem((count, part, width), lambda i: (0, 1, 0))],
        out_specs=vmem((count, part, width), lambda i: (0, 0, 0)),
        out_shape=jax.ShapeDtypeStruct((count, part, width), BF16),
        cost_estimate=cost(2 * joined.size, 2 * joined.size),
        compiler_params=pltpu.CompilerParams(vmem_limit_bytes=SMALL),
        name="scan_future",
    )(weights, joined)


def near_kernel(
    scale, weight_ref, query_ref, key_ref, value_ref, dmix_ref, gain_ref,
    mix_ref, grad_query_ref, grad_key_ref, grad_value_ref,
):
    rows = query_ref.shape[0]
    heads = gain_ref.shape[0] // pl.num_programs(0)
    dk, dv = query_ref.shape[1] // heads, value_ref.shape[1] // heads
    tiles = rows // TILE
    low = TILE.bit_length() - 1
    row = lax.broadcasted_iota(jnp.int32, (TILE, TILE), 0)
    column = lax.broadcasted_iota(jnp.int32, (TILE, TILE), 1)
    apart = row ^ column
    mixes, grad_queries, grad_keys, grad_values = {}, {}, {}, {}

    def add(sums, at, term):
        sums[at] = sums[at] + term if at in sums else term

    each = range(heads)
    names = [pl.program_id(0) * heads + h for h in each]
    gains = [column_of(gain_ref, names[h]) for h in each]
    tables = []
    for h in each:
        table = jnp.full((TILE, TILE), weight_ref[names[h], 0] * scale, F32)
        for level in range(1, low + 1):
            table = jnp.where(
                apart >= 2 ** (level - 1), weight_ref[names[h], level] * scale, table
            )
        tables.append(jnp.where(column <= row, table, F32(0.0)))
    for i in range(tiles):
        own = slice(i * TILE, (i + 1) * TILE)
        for j in range(i + 1):
            other = slice(j * TILE, (j + 1) * TILE)
            thin = [slice(h * dk, (h + 1) * dk) for h in each]
            wide = [slice(h * dv, (h + 1) * dv) for h in each]
            scores = [dot(query_ref[own, thin[h]], key_ref[other, thin[h]], CONTRACT_LAST) for h in each]
            slopes = [dot(dmix_ref[own, wide[h]], value_ref[other, wide[h]], CONTRACT_LAST) for h in each]
            pairs = [
                gains[h][own]
                * (tables[h] if i == j else weight_ref[names[h], low + (i ^ j).bit_length()] * scale)
                for h in each
            ]
            nears = [(pairs[h] * scores[h]).astype(BF16) for h in each]
            grads = [(pairs[h] * slopes[h]).astype(BF16) for h in each]
            for h in each:
                add(mixes, (h, i), dot(nears[h], value_ref[other, wide[h]]))
            for h in each:
                add(grad_queries, (h, i), dot(grads[h], key_ref[other, thin[h]]))
            for h in each:
                add(grad_values, (h, j), dot(nears[h], dmix_ref[own, wide[h]], CONTRACT_FIRST))
            for h in each:
                add(grad_keys, (h, j), dot(grads[h], query_ref[own, thin[h]], CONTRACT_FIRST))
        for h in each:
            mix_ref[own, h * dv : (h + 1) * dv] = mixes[h, i].astype(BF16)
            grad_query_ref[own, h * dk : (h + 1) * dk] = grad_queries[h, i].astype(BF16)
    for j in range(tiles):
        own = slice(j * TILE, (j + 1) * TILE)
        for h in each:
            grad_key_ref[own, h * dk : (h + 1) * dk] = grad_keys[h, j].astype(BF16)
            grad_value_ref[own, h * dv : (h + 1) * dv] = grad_values[h, j].astype(BF16)


def near_terms(queries, keys, values, dmix, gain, level_weights, scale, heads):
    rows, dk, dv = keys.shape[0], keys.shape[1] // heads, values.shape[1] // heads
    narrow = vmem((rows, STEP_HEADS * dk), lambda h: (0, h))
    wide = vmem((rows, STEP_HEADS * dv), lambda h: (0, h))
    thin, thick = (rows, heads * dk), (rows, heads * dv)
    return pl.pallas_call(
        functools.partial(near_kernel, scale),
        grid=(heads // STEP_HEADS,),
        in_specs=[smem(), narrow, narrow, wide, wide, vmem(gain.shape, lambda h: (0, 0))],
        out_specs=[wide, narrow, narrow, wide],
        out_shape=[pltpu.HBM(shape, BF16) for shape in (thick, thin, thin, thick)],
        cost_estimate=cost(1.5 * rows * rows * heads * 3 * (dk + dv), 8 * rows * heads * (dk + dv)),
        compiler_params=pltpu.CompilerParams(vmem_limit_bytes=LARGE),
        name="near_terms",
    )(level_weights, *in_hbm(queries, keys, values, dmix, gain))


def share_kernel(
    scale, heads, count, index_ref, query_hbm, own_ref, came_ref, mix_hbm, gain_ref, weight_hbm, *rest
):
    share_refs, (query, mix, weight, mixture, sems) = rest[: 2 * count], rest[2 * count :]
    rows, dk = query.shape[0], query.shape[1] // heads
    dv = own_ref.shape[1]
    each = rows // count
    half = weight.shape[1] // 2
    query_load = pltpu.make_async_copy(query_hbm, query, sems.at[0])
    mix_load = pltpu.make_async_copy(mix_hbm, mix, sems.at[1])
    sides = [
        pltpu.make_async_copy(
            weight_hbm.at[:, pl.ds(side * half, half)],
            weight.at[:, pl.ds(side * half, half)],
            sems.at[2 + side],
        )
        for side in range(2)
    ]
    for load in (query_load, mix_load, *sides):
        load.start()
    query_load.wait()
    mix_load.wait()
    for h in range(heads):
        past = state_of(index_ref[1], own_ref, came_ref, h, heads, dk)
        far = dot(query[:, h * dk : (h + 1) * dk], past)
        own = slice(h * dv, (h + 1) * dv)
        piece = (mix[:, own].astype(F32) + (column_of(gain_ref, h) * scale) * far).astype(BF16)
        for c in range(count):
            place = lax.rem(c + count - index_ref[0], count)
            at = pl.ds(pl.multiple_of(place * each, each), each)
            mixture[at, own] = piece[c * each : (c + 1) * each]
    for side in range(2):
        sides[side].wait()
        share = dot(mixture[...], weight[:, side * half : (side + 1) * half]).astype(BF16)
        for step in range(count):
            share_refs[side * count + step][...] = share[step * each : (step + 1) * each]


def shares_of(index, queries, own, came, mix, gain, weight, scale, heads, count):
    rows, dk = queries.shape[0], queries.shape[1] // heads
    dv, half = own.shape[1], weight.shape[1] // 2
    share = jax.ShapeDtypeStruct((rows // count, half), BF16)
    queries, mix, weight = in_hbm(queries, mix, weight)
    shares = pl.pallas_call(
        functools.partial(share_kernel, scale, heads, count),
        in_specs=[smem(), hbm(), vmem(), vmem(), hbm(), vmem(), hbm()],
        out_specs=[vmem()] * (2 * count),
        out_shape=[share] * (2 * count),
        scratch_shapes=[
            pltpu.VMEM(queries.shape, BF16),
            pltpu.VMEM(mix.shape, BF16),
            pltpu.VMEM(weight.shape, BF16),
            pltpu.VMEM(mix.shape, BF16),
            pltpu.SemaphoreType.DMA((4,)),
        ],
        cost_estimate=cost(2 * rows * dv * heads * (dk + 2 * half), 4 * half * (rows + heads * dv)),
        compiler_params=pltpu.CompilerParams(vmem_limit_bytes=LARGE),
        name="shares",
    )(index, queries, own, came, mix, gain, weight)
    return shares[:count], shares[count:]


def add_kernel(left_ref, right_ref, out_ref):
    out_ref[...] = (left_ref[...].astype(F32) + right_ref[...].astype(F32)).astype(BF16)


def added(left, right):
    return pl.pallas_call(
        add_kernel,
        in_specs=[vmem()] * 2,
        out_specs=vmem(),
        out_shape=jax.ShapeDtypeStruct(left.shape, BF16),
        cost_estimate=cost(left.size, 6 * left.size),
        compiler_params=pltpu.CompilerParams(vmem_limit_bytes=SMALL),
        name="added",
    )(left, right)


def total_kernel(*refs):
    *parts, out_ref = refs
    half = parts[0].shape[1]
    for side in range(2):
        a, b, c = (ref[...].astype(F32) for ref in parts[3 * side : 3 * side + 3])
        out_ref[:, side * half : (side + 1) * half] = (a + b + c).astype(BF16)


def total(*parts):
    rows, half = parts[0].shape
    return pl.pallas_call(
        total_kernel,
        in_specs=[vmem()] * 6,
        out_specs=vmem(),
        out_shape=jax.ShapeDtypeStruct((rows, 2 * half), BF16),
        cost_estimate=cost(4 * rows * half, 16 * rows * half),
        compiler_params=pltpu.CompilerParams(vmem_limit_bytes=SMALL),
        name="total",
    )(*parts)


def far_past_kernel(
    scale, heads, core_ref, dmix_hbm, gain_ref, own_ref, came_ref, near_hbm, grad_hbm,
    dmix, near, grad, sems,
):
    dk, dv = near.shape[1] // heads, dmix.shape[1] // heads
    loads, stores = [], []
    for h in range(heads):
        for n, (source, target, size) in enumerate(((dmix_hbm, dmix, dv), (near_hbm, near, dk))):
            at = pl.ds(h * size, size)
            loads.append(pltpu.make_async_copy(source.at[:, at], target.at[:, at], sems.at[n, h]))
            loads[-1].start()
    for h in range(heads):
        past = state_of(core_ref[0], own_ref, came_ref, h, heads, dk)
        for load in loads[2 * h : 2 * h + 2]:
            load.wait()
        far = dot(dmix[:, h * dv : (h + 1) * dv], past, CONTRACT_LAST)
        own, at = slice(h * dk, (h + 1) * dk), pl.ds(h * dk, dk)
        total = near[:, own].astype(F32) + (column_of(gain_ref, h) * scale) * far
        grad[:, own] = total.astype(BF16)
        stores.append(pltpu.make_async_copy(grad.at[:, at], grad_hbm.at[:, at], sems.at[2, h]))
        stores[-1].start()
    for store in stores:
        store.wait()


def far_past(core, dmix, gain, own, came, near, scale, heads):
    rows, dk, dv = near.shape[0], near.shape[1] // heads, dmix.shape[1] // heads
    dmix, near = in_hbm(dmix, near)
    return pl.pallas_call(
        functools.partial(far_past_kernel, scale, heads),
        in_specs=[smem(), hbm(), vmem(), vmem(), vmem(), hbm()],
        out_specs=hbm(),
        out_shape=pltpu.HBM(near.shape, BF16),
        scratch_shapes=[
            pltpu.VMEM(dmix.shape, BF16),
            pltpu.VMEM(near.shape, BF16),
            pltpu.VMEM(near.shape, BF16),
            pltpu.SemaphoreType.DMA((3, heads)),
        ],
        cost_estimate=cost(2 * rows * dk * dv * heads, 2 * rows * heads * (2 * dk + dv)),
        compiler_params=pltpu.CompilerParams(vmem_limit_bytes=SMALL),
        name="far_past",
    )(core, dmix, gain, own, came, near)


def far_future_kernel(
    scale, heads, core_ref, key_hbm, value_hbm, own_ref, came_ref, near_key_hbm, near_value_hbm,
    grad_key_hbm, grad_value_hbm, key, value, near_key, near_value, grad_key, grad_value, sems,
):
    dk, dv = key.shape[1] // heads, value.shape[1] // heads
    loads, stores = [], []
    for h in range(heads):
        thin, thick = pl.ds(h * dk, dk), pl.ds(h * dv, dv)
        for n, (source, target, at) in enumerate(
            (
                (value_hbm, value, thick),
                (near_key_hbm, near_key, thin),
                (key_hbm, key, thin),
                (near_value_hbm, near_value, thick),
            )
        ):
            loads.append(pltpu.make_async_copy(source.at[:, at], target.at[:, at], sems.at[n, h]))
    for load in loads:
        load.start()
    for h in range(heads):
        thin, thick = pl.ds(h * dk, dk), pl.ds(h * dv, dv)
        narrow, wide = slice(h * dk, (h + 1) * dk), slice(h * dv, (h + 1) * dv)
        future = state_of(core_ref[0], own_ref, came_ref, h, heads, dk)
        for load in loads[4 * h : 4 * h + 2]:
            load.wait()
        far_key = dot(value[:, wide], future, CONTRACT_LAST)
        grad_key[:, narrow] = (near_key[:, narrow].astype(F32) + scale * far_key).astype(BF16)
        stores.append(
            pltpu.make_async_copy(grad_key.at[:, thin], grad_key_hbm.at[:, thin], sems.at[4, h])
        )
        stores[-1].start()
        for load in loads[4 * h + 2 : 4 * h + 4]:
            load.wait()
        far_value = dot(key[:, narrow], future)
        grad_value[:, wide] = (near_value[:, wide].astype(F32) + scale * far_value).astype(BF16)
        stores.append(
            pltpu.make_async_copy(grad_value.at[:, thick], grad_value_hbm.at[:, thick], sems.at[5, h])
        )
        stores[-1].start()
    for store in stores:
        store.wait()


def far_future(core, keys, values, own, came, near_keys, near_values, scale, heads):
    rows, dk, dv = keys.shape[0], keys.shape[1] // heads, values.shape[1] // heads
    thin, thick = keys.shape, values.shape
    keys, values, near_keys, near_values = in_hbm(keys, values, near_keys, near_values)
    return pl.pallas_call(
        functools.partial(far_future_kernel, scale, heads),
        in_specs=[smem(), hbm(), hbm(), vmem(), vmem(), hbm(), hbm()],
        out_specs=[hbm()] * 2,
        out_shape=[pltpu.HBM(thin, BF16), pltpu.HBM(thick, BF16)],
        scratch_shapes=[
            pltpu.VMEM(shape, BF16) for shape in (thin, thick, thin, thick, thin, thick)
        ]
        + [pltpu.SemaphoreType.DMA((6, heads))],
        cost_estimate=cost(4 * rows * dk * dv * heads, 6 * rows * heads * (dk + dv)),
        compiler_params=pltpu.CompilerParams(vmem_limit_bytes=LARGE),
        name="far_future",
    )(core, keys, values, own, came, near_keys, near_values)


def swapped(pieces, axis, groups):
    return lax.all_to_all(
        pieces, axis, split_axis=0, concat_axis=0, tiled=True, axis_index_groups=groups
    )


def from_sibling(value, axis):
    return lax.ppermute(value, axis, [(i, i ^ 1) for i in range(lax.axis_size(axis))])


def turned(value, axis, step):
    count = lax.axis_size(axis)
    return lax.ppermute(value, axis, [(i, (i + step) % count) for i in range(count)])


def summed_shares(left, right, axis):
    left_far = turned(left[2], axis, 1)
    right_far = turned(right[2], axis, -1)
    left_back = turned(left[3], axis, -1)
    right_on = turned(right[1], axis, 1)
    left_on = turned(added(left[1], left_far), axis, 1)
    right_back = turned(added(right[3], right_far), axis, -1)
    return total(left[0], left_on, left_back, right[0], right_on, right_back)


def on_device(
    query_vectors, key_vectors, value_vectors, query_gain, level_gain, out_weight, out_grad
):
    heads, rows = query_gain.shape
    dk = query_vectors.shape[1] // heads
    scale = dk ** (-0.5)
    seq_count = lax.axis_size("seq")
    bits = seq_count.bit_length() - 1
    shift_bits = rows.bit_length() - 1
    level_weights = level_weights_of(level_gain)
    gain = query_gain
    chips = seq_count // 2
    groups = [[2 * chip + core for chip in range(chips)] for core in range(2)]
    chip, core = lax.axis_index("seq") // 2, lax.axis_index("seq") % 2
    head = core * (heads // 2) + chip * (heads // 2) // chips
    scan_weights = lax.dynamic_slice(level_weights, (head, shift_bits + 2), (1, bits - 1))
    pair_weights = lax.dynamic_slice(
        level_weights, (core * (heads // 2), shift_bits + 1), (heads // 2, 1)
    )
    index = jnp.stack([lax.axis_index("head"), core])
    core = core.reshape(1)

    key_mine, key_sent = key_state(core, key_vectors, value_vectors, heads)
    key_other = from_sibling(key_sent, "seq")
    key_pieces = swapped(chip_sum(key_mine, key_other, chips), "seq", groups)
    dmix, query_mine, query_sent = mix_grad(core, out_grad, out_weight, query_vectors, gain, heads)
    query_other = from_sibling(query_sent, "seq")
    past_pieces = scan_past(key_pieces, query_mine, query_other, scan_weights)
    joined = swapped(past_pieces, "seq", groups)
    mix, near_queries, near_keys, near_values = near_terms(
        query_vectors, key_vectors, value_vectors, dmix, gain, level_weights, scale, heads
    )
    past_own, past_sent = parts_of(core, pair_weights, joined, key_mine, key_other, True)
    past_came = from_sibling(past_sent, "seq")
    left, right = shares_of(
        index, query_vectors, past_own, past_came, mix, gain, out_weight, scale, heads,
        lax.axis_size("head"),
    )
    layer_out = summed_shares(left, right, "head")
    grad_queries = far_past(core, dmix, gain, past_own, past_came, near_queries, scale, heads)
    future_pieces = scan_future(joined, scan_weights)
    future = swapped(future_pieces, "seq", groups)
    future_own, future_sent = parts_of(core, pair_weights, future, query_mine, query_other, False)
    future_came = from_sibling(future_sent, "seq")
    grad_keys, grad_values = far_future(
        core, key_vectors, value_vectors, future_own, future_came, near_keys, near_values,
        scale, heads,
    )
    return (layer_out, grad_queries, grad_keys, grad_values)


def solution(mesh):
    return jax.shard_map(
        on_device,
        mesh=mesh,
        in_specs=(
            P("seq", "head"),
            P("seq", "head"),
            P("seq", "head"),
            P("head", "seq"),
            P("head", None),
            P("head", None),
            P("seq", None),
        ),
        out_specs=(P(("seq", "head"), None), P("seq", "head"), P("seq", "head"), P("seq", "head")),
        check_vma=False,
    )
```

```python
import functools

import jax
import jax.numpy as jnp
from jax import lax
from jax.experimental import pallas as pl
from jax.experimental.pallas import tpu as pltpu
from jax.sharding import PartitionSpec as P


F32 = jnp.float32
BF16 = jnp.bfloat16
CONTRACT_LAST = (((1,), (1,)), ((), ()))
CONTRACT_FIRST = (((0,), (0,)), ((), ()))
PLAIN = (((1,), (0,)), ((), ()))
TILE = 256
STEP_HEADS = 2
SMALL = 8 * 2**20
LARGE = 24 * 2**20


def dot(left, right, dims=PLAIN):
    return lax.dot_general(left, right, dims, preferred_element_type=F32)


def vmem(shape=None, index_map=None):
    if shape is None:
        return pl.BlockSpec(memory_space=pltpu.VMEM)
    return pl.BlockSpec(shape, index_map)


def hbm():
    return pl.BlockSpec(memory_space=pltpu.HBM)


def in_hbm(*arrays):
    return [pltpu.with_memory_space_constraint(array, pltpu.HBM) for array in arrays]


def column_of(gain_ref, head):
    row = gain_ref[pl.ds(head, 1)]
    return jnp.transpose(jnp.broadcast_to(row, (8, row.shape[1])), (1, 0))[:, :1]


def smem():
    return pl.BlockSpec(memory_space=pltpu.SMEM)


def cost(flops, moved):
    return pl.CostEstimate(flops=int(flops), bytes_accessed=int(moved), transcendentals=0)


def level_weights_of(level_gain):
    levels = jnp.arange(level_gain.shape[1], dtype=jnp.int32)
    decline = jnp.exp2(-0.5 * (levels - 1).astype(F32))
    factor = jnp.where(levels == 0, F32(1.0), decline)
    return level_gain * factor[None, :]


def key_state_kernel(
    heads, core_ref, key_hbm, value_hbm, mine_ref, other_ref, key, value, state, sems
):
    dk, dv = key.shape[1] // heads, value.shape[1] // heads
    loads = []
    for h in range(heads):
        narrow, wide = pl.ds(h * dk, dk), pl.ds(h * dv, dv)
        loads.append(
            (
                pltpu.make_async_copy(key_hbm.at[:, narrow], key.at[:, narrow], sems.at[0, h]),
                pltpu.make_async_copy(value_hbm.at[:, wide], value.at[:, wide], sems.at[1, h]),
            )
        )
    for pair in loads:
        for load in pair:
            load.start()
    for h in range(heads):
        for load in loads[h]:
            load.wait()
        narrow, wide = slice(h * dk, (h + 1) * dk), slice(h * dv, (h + 1) * dv)
        state[narrow] = dot(key[:, narrow], value[:, wide], CONTRACT_FIRST).astype(BF16)
    take_halves(core_ref, state, mine_ref, other_ref)


def take_halves(core_ref, state, mine_ref, other_ref):
    half = mine_ref.shape[0]
    mine_ref[...] = state[pl.ds(pl.multiple_of(core_ref[0] * half, half), half)]
    other_ref[...] = state[pl.ds(pl.multiple_of((1 - core_ref[0]) * half, half), half)]


def key_state(core, keys, values, heads):
    rows, dk, dv = keys.shape[0], keys.shape[1] // heads, values.shape[1] // heads
    return pl.pallas_call(
        functools.partial(key_state_kernel, heads),
        in_specs=[smem(), hbm(), hbm()],
        out_specs=[vmem()] * 2,
        out_shape=[jax.ShapeDtypeStruct((heads * dk // 2, dv), BF16)] * 2,
        scratch_shapes=[
            pltpu.VMEM(keys.shape, BF16),
            pltpu.VMEM(values.shape, BF16),
            pltpu.VMEM((heads * dk, dv), BF16),
            pltpu.SemaphoreType.DMA((2, heads)),
        ],
        cost_estimate=cost(2 * rows * dk * dv * heads, 2 * rows * (dk + dv) * heads),
        compiler_params=pltpu.CompilerParams(vmem_limit_bytes=SMALL),
        name="key_state",
    )(core, *in_hbm(keys, values))


def mix_grad_kernel(
    heads, core_ref, grad_hbm, weight_hbm, query_hbm, gain_hbm, dmix_hbm, mine_ref, other_ref,
    dmix, grad, weight, query, state, gain_ref, sems,
):
    dk, dv = query.shape[1] // heads, weight.shape[0] // heads
    pair = 2 * dv

    def started(number, source, target):
        copy = pltpu.make_async_copy(source, target, sems.at[number])
        copy.start()
        return copy

    depth = grad.shape[1] // 3
    firsts = []
    for n in range(3):
        at = pl.ds(n * depth, depth)
        firsts.append(
            (
                started(2 * n, grad_hbm.at[:, at], grad.at[:, at]),
                started(2 * n + 1, weight_hbm.at[pl.ds(0, pair), at], weight.at[pl.ds(0, pair), at]),
            )
        )
    query_load = started(6, query_hbm, query)
    gain_load = started(6 + heads, gain_hbm, gain_ref)
    loads = [None] + [
        started(6 + n, weight_hbm.at[pl.ds(n * pair, pair)], weight.at[pl.ds(n * pair, pair)])
        for n in range(1, heads // 2)
    ]
    base = 6 + heads // 2
    stores = []
    for n in range(heads // 2):
        both = slice(n * pair, (n + 1) * pair)
        if n == 0:
            piece = None
            for step, copies in enumerate(firsts):
                for copy in copies:
                    copy.wait()
                at = slice(step * depth, (step + 1) * depth)
                term = dot(grad[:, at], weight[both, at], CONTRACT_LAST)
                piece = term if piece is None else piece + term
        else:
            loads[n].wait()
            piece = dot(grad[...], weight[both], CONTRACT_LAST)
        piece = piece.astype(BF16)
        dmix[:, both] = piece
        at = pl.ds(n * pair, pair)
        stores.append(started(base + n, dmix.at[:, at], dmix_hbm.at[:, at]))
        if n == 0:
            query_load.wait()
            gain_load.wait()
        for h in (2 * n, 2 * n + 1):
            own = piece[:, (h - 2 * n) * dv : (h - 2 * n + 1) * dv].astype(F32)
            gained = (own * column_of(gain_ref, h)).astype(BF16)
            rows = slice(h * dk, (h + 1) * dk)
            state[rows] = dot(query[:, rows], gained, CONTRACT_FIRST).astype(BF16)
    take_halves(core_ref, state, mine_ref, other_ref)
    for store in stores:
        store.wait()


def mix_grad(core, out_grad, out_weight, queries, gain, heads):
    rows, width = out_grad.shape
    dv, dk = out_weight.shape[0] // heads, queries.shape[1] // heads
    return pl.pallas_call(
        functools.partial(mix_grad_kernel, heads),
        in_specs=[smem(), hbm(), hbm(), hbm(), hbm()],
        out_specs=[hbm(), vmem(), vmem()],
        out_shape=[
            pltpu.HBM((rows, heads * dv), BF16),
            jax.ShapeDtypeStruct((heads * dk // 2, dv), BF16),
            jax.ShapeDtypeStruct((heads * dk // 2, dv), BF16),
        ],
        scratch_shapes=[
            pltpu.VMEM((rows, heads * dv), BF16),
            pltpu.VMEM(out_grad.shape, BF16),
            pltpu.VMEM(out_weight.shape, BF16),
            pltpu.VMEM(queries.shape, BF16),
            pltpu.VMEM((heads * dk, dv), BF16),
            pltpu.VMEM(gain.shape, F32),
            pltpu.SemaphoreType.DMA((7 + heads,)),
        ],
        cost_estimate=cost(2 * rows * dv * heads * (width + dk), 2 * (rows + dv * heads) * width),
        compiler_params=pltpu.CompilerParams(vmem_limit_bytes=LARGE),
        name="mix_grad",
    )(core, *in_hbm(out_grad, out_weight, queries, gain))


def scan_pieces(earlier, weight_ref, pieces_ref, write):
    count = pieces_ref.shape[0]
    bits = count.bit_length() - 1
    groups = [[pieces_ref[c].astype(F32) for c in range(count)]]
    for _ in range(bits - 1):
        below = groups[-1]
        groups.append([below[2 * g] + below[2 * g + 1] for g in range(len(below) // 2)])
    carried = [None]
    for bit in reversed(range(bits)):
        weight = weight_ref[0, bit]
        spread = []
        for g, carry in enumerate(carried):
            other = groups[bit][2 * g if earlier else 2 * g + 1] * weight
            total = other if carry is None else carry + other
            spread += [carry, total] if earlier else [total, carry]
        carried = spread
    for c, total in enumerate(carried):
        value = jnp.zeros(pieces_ref.shape[1:], F32) if total is None else total
        write(c, value.astype(BF16))


def chip_sum_kernel(mine_ref, other_ref, sum_ref):
    part = sum_ref.shape[1]
    for c in range(sum_ref.shape[0]):
        own = slice(c * part, (c + 1) * part)
        sum_ref[c] = (mine_ref[own].astype(F32) + other_ref[own].astype(F32)).astype(BF16)


def chip_sum(mine, other, count):
    return pl.pallas_call(
        chip_sum_kernel,
        in_specs=[vmem()] * 2,
        out_specs=vmem(),
        out_shape=jax.ShapeDtypeStruct((count, mine.shape[0] // count, mine.shape[1]), BF16),
        cost_estimate=cost(mine.size, 6 * mine.size),
        compiler_params=pltpu.CompilerParams(vmem_limit_bytes=SMALL),
        name="chip_sum",
    )(mine, other)


def scan_past_kernel(weight_ref, pieces_ref, mine_ref, other_ref, joined_ref):
    part = pieces_ref.shape[1]

    def write(c, value):
        own = slice(c * part, (c + 1) * part)
        query = mine_ref[own].astype(F32) + other_ref[own].astype(F32)
        joined_ref[c, :part] = value
        joined_ref[c, part:] = query.astype(BF16)

    scan_pieces(True, weight_ref, pieces_ref, write)


def scan_past(pieces, mine, other, weights):
    count, part, width = pieces.shape
    return pl.pallas_call(
        scan_past_kernel,
        in_specs=[smem()] + [vmem()] * 3,
        out_specs=vmem(),
        out_shape=jax.ShapeDtypeStruct((count, 2 * part, width), BF16),
        cost_estimate=cost(4 * pieces.size, 8 * pieces.size),
        compiler_params=pltpu.CompilerParams(vmem_limit_bytes=SMALL),
        name="scan_past",
    )(weights, pieces, mine, other)


def parts_kernel(earlier, core_ref, weight_ref, shared_ref, mine_ref, other_ref, own_ref, sent_ref):
    part = mine_ref.shape[0] // shared_ref.shape[0]
    heads = weight_ref.shape[0]
    each = mine_ref.shape[0] // heads
    upper = core_ref[0] == 1
    owns = upper if earlier else jnp.logical_not(upper)
    for h in range(heads):
        at = slice(h * each, (h + 1) * each)
        held = slice(h * each // part, (h + 1) * each // part)
        shared = shared_ref[held, :part].reshape(each, -1).astype(F32)
        weight = weight_ref[h, 0]
        with_other = (shared + weight * other_ref[at].astype(F32)).astype(BF16)
        with_mine = (shared + weight * mine_ref[at].astype(F32)).astype(BF16)
        plain = shared.astype(BF16)
        own_ref[at] = jnp.where(owns, with_other, plain)
        sent_ref[at] = jnp.where(owns, plain, with_mine)


def parts_of(core, weights, shared, mine, other, earlier):
    return pl.pallas_call(
        functools.partial(parts_kernel, earlier),
        in_specs=[smem()] * 2 + [vmem()] * 3,
        out_specs=[vmem()] * 2,
        out_shape=[jax.ShapeDtypeStruct(mine.shape, BF16)] * 2,
        cost_estimate=cost(4 * mine.size, 10 * mine.size),
        compiler_params=pltpu.CompilerParams(vmem_limit_bytes=SMALL),
        name="past_parts" if earlier else "future_parts",
    )(core, weights, shared, mine, other)


def state_of(core, own_ref, came_ref, h, heads, dk):
    at = h % (heads // 2)
    own, came = own_ref[at * dk : (at + 1) * dk], came_ref[at * dk : (at + 1) * dk]
    return jnp.where(core == h // (heads // 2), own, came)


def scan_future_kernel(weight_ref, pieces_ref, sums_ref):
    def write(c, value):
        sums_ref[c] = value

    scan_pieces(False, weight_ref, pieces_ref, write)


def scan_future(joined, weights):
    count, part, width = joined.shape
    part = part // 2
    return pl.pallas_call(
        scan_future_kernel,
        grid=(1,),
        in_specs=[smem(), vmem((count, part, width), lambda i: (0, 1, 0))],
        out_specs=vmem((count, part, width), lambda i: (0, 0, 0)),
        out_shape=jax.ShapeDtypeStruct((count, part, width), BF16),
        cost_estimate=cost(2 * joined.size, 2 * joined.size),
        compiler_params=pltpu.CompilerParams(vmem_limit_bytes=SMALL),
        name="scan_future",
    )(weights, joined)


def near_kernel(
    scale, weight_ref, query_ref, key_ref, value_ref, dmix_ref, gain_ref,
    mix_ref, grad_query_ref, grad_key_ref, grad_value_ref,
):
    rows = query_ref.shape[0]
    heads = gain_ref.shape[0] // pl.num_programs(0)
    dk, dv = query_ref.shape[1] // heads, value_ref.shape[1] // heads
    tiles = rows // TILE
    low = TILE.bit_length() - 1
    row = lax.broadcasted_iota(jnp.int32, (TILE, TILE), 0)
    column = lax.broadcasted_iota(jnp.int32, (TILE, TILE), 1)
    apart = row ^ column
    mixes, grad_queries, grad_keys, grad_values = {}, {}, {}, {}

    def add(sums, at, term):
        sums[at] = sums[at] + term if at in sums else term

    each = range(heads)
    names = [pl.program_id(0) * heads + h for h in each]
    gains = [column_of(gain_ref, names[h]) for h in each]
    tables = []
    for h in each:
        table = jnp.full((TILE, TILE), weight_ref[names[h], 0] * scale, F32)
        for level in range(1, low + 1):
            table = jnp.where(
                apart >= 2 ** (level - 1), weight_ref[names[h], level] * scale, table
            )
        tables.append(jnp.where(column <= row, table, F32(0.0)))
    for i in range(tiles):
        own = slice(i * TILE, (i + 1) * TILE)
        for j in range(i + 1):
            other = slice(j * TILE, (j + 1) * TILE)
            thin = [slice(h * dk, (h + 1) * dk) for h in each]
            wide = [slice(h * dv, (h + 1) * dv) for h in each]
            scores = [dot(query_ref[own, thin[h]], key_ref[other, thin[h]], CONTRACT_LAST) for h in each]
            slopes = [dot(dmix_ref[own, wide[h]], value_ref[other, wide[h]], CONTRACT_LAST) for h in each]
            pairs = [
                gains[h][own]
                * (tables[h] if i == j else weight_ref[names[h], low + (i ^ j).bit_length()] * scale)
                for h in each
            ]
            nears = [(pairs[h] * scores[h]).astype(BF16) for h in each]
            grads = [(pairs[h] * slopes[h]).astype(BF16) for h in each]
            for h in each:
                add(mixes, (h, i), dot(nears[h], value_ref[other, wide[h]]))
            for h in each:
                add(grad_queries, (h, i), dot(grads[h], key_ref[other, thin[h]]))
            for h in each:
                add(grad_values, (h, j), dot(nears[h], dmix_ref[own, wide[h]], CONTRACT_FIRST))
            for h in each:
                add(grad_keys, (h, j), dot(grads[h], query_ref[own, thin[h]], CONTRACT_FIRST))
        for h in each:
            mix_ref[own, h * dv : (h + 1) * dv] = mixes[h, i].astype(BF16)
            grad_query_ref[own, h * dk : (h + 1) * dk] = grad_queries[h, i].astype(BF16)
    for j in range(tiles):
        own = slice(j * TILE, (j + 1) * TILE)
        for h in each:
            grad_key_ref[own, h * dk : (h + 1) * dk] = grad_keys[h, j].astype(BF16)
            grad_value_ref[own, h * dv : (h + 1) * dv] = grad_values[h, j].astype(BF16)


def near_terms(queries, keys, values, dmix, gain, level_weights, scale, heads):
    rows, dk, dv = keys.shape[0], keys.shape[1] // heads, values.shape[1] // heads
    narrow = vmem((rows, STEP_HEADS * dk), lambda h: (0, h))
    wide = vmem((rows, STEP_HEADS * dv), lambda h: (0, h))
    thin, thick = (rows, heads * dk), (rows, heads * dv)
    return pl.pallas_call(
        functools.partial(near_kernel, scale),
        grid=(heads // STEP_HEADS,),
        in_specs=[smem(), narrow, narrow, wide, wide, vmem(gain.shape, lambda h: (0, 0))],
        out_specs=[wide, narrow, narrow, wide],
        out_shape=[pltpu.HBM(shape, BF16) for shape in (thick, thin, thin, thick)],
        cost_estimate=cost(1.5 * rows * rows * heads * 3 * (dk + dv), 8 * rows * heads * (dk + dv)),
        compiler_params=pltpu.CompilerParams(vmem_limit_bytes=LARGE),
        name="near_terms",
    )(level_weights, *in_hbm(queries, keys, values, dmix, gain))


def share_kernel(
    scale, heads, count, index_ref, query_hbm, own_ref, came_ref, mix_hbm, gain_ref, weight_hbm, *rest
):
    share_refs, (query, mix, weight, mixture, sems) = rest[: 2 * count], rest[2 * count :]
    rows, dk = query.shape[0], query.shape[1] // heads
    dv = own_ref.shape[1]
    each = rows // count
    half = weight.shape[1] // 2
    cut = -(-half // TILE) * TILE
    spans = ((0, cut), (cut, 2 * half))
    query_load = pltpu.make_async_copy(query_hbm, query, sems.at[0])
    mix_load = pltpu.make_async_copy(mix_hbm, mix, sems.at[1])
    sides = [
        pltpu.make_async_copy(
            weight_hbm.at[:, pl.ds(start, stop - start)],
            weight.at[:, pl.ds(start, stop - start)],
            sems.at[2 + side],
        )
        for side, (start, stop) in enumerate(spans)
    ]
    for load in (query_load, mix_load, *sides):
        load.start()
    query_load.wait()
    mix_load.wait()
    for h in range(heads):
        past = state_of(index_ref[1], own_ref, came_ref, h, heads, dk)
        far = dot(query[:, h * dk : (h + 1) * dk], past)
        own = slice(h * dv, (h + 1) * dv)
        piece = (mix[:, own].astype(F32) + (column_of(gain_ref, h) * scale) * far).astype(BF16)
        for c in range(count):
            place = lax.rem(c + count - index_ref[0], count)
            at = pl.ds(pl.multiple_of(place * each, each), each)
            mixture[at, own] = piece[c * each : (c + 1) * each]
    for side, (start, stop) in enumerate(spans):
        sides[side].wait()
        share = dot(mixture[...], weight[:, start:stop]).astype(BF16)
        for step in range(count):
            part = share[step * each : (step + 1) * each]
            if side == 0:
                share_refs[step][...] = part[:, :half]
                share_refs[count + step][:, : cut - half] = part[:, half:]
            else:
                share_refs[count + step][:, cut - half :] = part


def shares_of(index, queries, own, came, mix, gain, weight, scale, heads, count):
    rows, dk = queries.shape[0], queries.shape[1] // heads
    dv, half = own.shape[1], weight.shape[1] // 2
    share = jax.ShapeDtypeStruct((rows // count, half), BF16)
    queries, mix, weight = in_hbm(queries, mix, weight)
    shares = pl.pallas_call(
        functools.partial(share_kernel, scale, heads, count),
        in_specs=[smem(), hbm(), vmem(), vmem(), hbm(), vmem(), hbm()],
        out_specs=[vmem()] * (2 * count),
        out_shape=[share] * (2 * count),
        scratch_shapes=[
            pltpu.VMEM(queries.shape, BF16),
            pltpu.VMEM(mix.shape, BF16),
            pltpu.VMEM(weight.shape, BF16),
            pltpu.VMEM(mix.shape, BF16),
            pltpu.SemaphoreType.DMA((4,)),
        ],
        cost_estimate=cost(2 * rows * dv * heads * (dk + 2 * half), 4 * half * (rows + heads * dv)),
        compiler_params=pltpu.CompilerParams(vmem_limit_bytes=LARGE),
        name="shares",
    )(index, queries, own, came, mix, gain, weight)
    return shares[:count], shares[count:]


def add_kernel(left_ref, right_ref, out_ref):
    out_ref[...] = (left_ref[...].astype(F32) + right_ref[...].astype(F32)).astype(BF16)


def added(left, right):
    return pl.pallas_call(
        add_kernel,
        in_specs=[vmem()] * 2,
        out_specs=vmem(),
        out_shape=jax.ShapeDtypeStruct(left.shape, BF16),
        cost_estimate=cost(left.size, 6 * left.size),
        compiler_params=pltpu.CompilerParams(vmem_limit_bytes=SMALL),
        name="added",
    )(left, right)


def total_kernel(*refs):
    *parts, out_ref = refs
    half = parts[0].shape[1]
    for side in range(2):
        a, b, c = (ref[...].astype(F32) for ref in parts[3 * side : 3 * side + 3])
        out_ref[:, side * half : (side + 1) * half] = (a + b + c).astype(BF16)


def total(*parts):
    rows, half = parts[0].shape
    return pl.pallas_call(
        total_kernel,
        in_specs=[vmem()] * 6,
        out_specs=vmem(),
        out_shape=jax.ShapeDtypeStruct((rows, 2 * half), BF16),
        cost_estimate=cost(4 * rows * half, 16 * rows * half),
        compiler_params=pltpu.CompilerParams(vmem_limit_bytes=SMALL),
        name="total",
    )(*parts)


def far_past_kernel(
    scale, heads, core_ref, dmix_hbm, gain_ref, own_ref, came_ref, near_hbm, grad_hbm,
    dmix, near, grad, sems,
):
    dk, dv = near.shape[1] // heads, dmix.shape[1] // heads
    loads, stores = [], []
    for h in range(heads):
        for n, (source, target, size) in enumerate(((dmix_hbm, dmix, dv), (near_hbm, near, dk))):
            at = pl.ds(h * size, size)
            loads.append(pltpu.make_async_copy(source.at[:, at], target.at[:, at], sems.at[n, h]))
            loads[-1].start()
    for h in range(heads):
        past = state_of(core_ref[0], own_ref, came_ref, h, heads, dk)
        for load in loads[2 * h : 2 * h + 2]:
            load.wait()
        far = dot(dmix[:, h * dv : (h + 1) * dv], past, CONTRACT_LAST)
        own, at = slice(h * dk, (h + 1) * dk), pl.ds(h * dk, dk)
        total = near[:, own].astype(F32) + (column_of(gain_ref, h) * scale) * far
        grad[:, own] = total.astype(BF16)
        stores.append(pltpu.make_async_copy(grad.at[:, at], grad_hbm.at[:, at], sems.at[2, h]))
        stores[-1].start()
    for store in stores:
        store.wait()


def far_past(core, dmix, gain, own, came, near, scale, heads):
    rows, dk, dv = near.shape[0], near.shape[1] // heads, dmix.shape[1] // heads
    dmix, near = in_hbm(dmix, near)
    return pl.pallas_call(
        functools.partial(far_past_kernel, scale, heads),
        in_specs=[smem(), hbm(), vmem(), vmem(), vmem(), hbm()],
        out_specs=hbm(),
        out_shape=pltpu.HBM(near.shape, BF16),
        scratch_shapes=[
            pltpu.VMEM(dmix.shape, BF16),
            pltpu.VMEM(near.shape, BF16),
            pltpu.VMEM(near.shape, BF16),
            pltpu.SemaphoreType.DMA((3, heads)),
        ],
        cost_estimate=cost(2 * rows * dk * dv * heads, 2 * rows * heads * (2 * dk + dv)),
        compiler_params=pltpu.CompilerParams(vmem_limit_bytes=SMALL),
        name="far_past",
    )(core, dmix, gain, own, came, near)


def far_future_kernel(
    scale, heads, core_ref, key_hbm, value_hbm, own_ref, came_ref, near_key_hbm, near_value_hbm,
    grad_key_hbm, grad_value_hbm, key, value, near_key, near_value, grad_key, grad_value, sems,
):
    dk, dv = key.shape[1] // heads, value.shape[1] // heads
    loads, stores = [], []
    for h in range(heads):
        thin, thick = pl.ds(h * dk, dk), pl.ds(h * dv, dv)
        for n, (source, target, at) in enumerate(
            (
                (value_hbm, value, thick),
                (near_key_hbm, near_key, thin),
                (key_hbm, key, thin),
                (near_value_hbm, near_value, thick),
            )
        ):
            loads.append(pltpu.make_async_copy(source.at[:, at], target.at[:, at], sems.at[n, h]))
    for load in loads:
        load.start()
    for h in range(heads):
        thin, thick = pl.ds(h * dk, dk), pl.ds(h * dv, dv)
        narrow, wide = slice(h * dk, (h + 1) * dk), slice(h * dv, (h + 1) * dv)
        future = state_of(core_ref[0], own_ref, came_ref, h, heads, dk)
        for load in loads[4 * h : 4 * h + 2]:
            load.wait()
        far_key = dot(value[:, wide], future, CONTRACT_LAST)
        grad_key[:, narrow] = (near_key[:, narrow].astype(F32) + scale * far_key).astype(BF16)
        stores.append(
            pltpu.make_async_copy(grad_key.at[:, thin], grad_key_hbm.at[:, thin], sems.at[4, h])
        )
        stores[-1].start()
        for load in loads[4 * h + 2 : 4 * h + 4]:
            load.wait()
        far_value = dot(key[:, narrow], future)
        grad_value[:, wide] = (near_value[:, wide].astype(F32) + scale * far_value).astype(BF16)
        stores.append(
            pltpu.make_async_copy(grad_value.at[:, thick], grad_value_hbm.at[:, thick], sems.at[5, h])
        )
        stores[-1].start()
    for store in stores:
        store.wait()


def far_future(core, keys, values, own, came, near_keys, near_values, scale, heads):
    rows, dk, dv = keys.shape[0], keys.shape[1] // heads, values.shape[1] // heads
    thin, thick = keys.shape, values.shape
    keys, values, near_keys, near_values = in_hbm(keys, values, near_keys, near_values)
    return pl.pallas_call(
        functools.partial(far_future_kernel, scale, heads),
        in_specs=[smem(), hbm(), hbm(), vmem(), vmem(), hbm(), hbm()],
        out_specs=[hbm()] * 2,
        out_shape=[pltpu.HBM(thin, BF16), pltpu.HBM(thick, BF16)],
        scratch_shapes=[
            pltpu.VMEM(shape, BF16) for shape in (thin, thick, thin, thick, thin, thick)
        ]
        + [pltpu.SemaphoreType.DMA((6, heads))],
        cost_estimate=cost(4 * rows * dk * dv * heads, 6 * rows * heads * (dk + dv)),
        compiler_params=pltpu.CompilerParams(vmem_limit_bytes=LARGE),
        name="far_future",
    )(core, keys, values, own, came, near_keys, near_values)


def swapped(pieces, axis, groups):
    return lax.all_to_all(
        pieces, axis, split_axis=0, concat_axis=0, tiled=True, axis_index_groups=groups
    )


def from_sibling(value, axis):
    return lax.ppermute(value, axis, [(i, i ^ 1) for i in range(lax.axis_size(axis))])


def turned(value, axis, step):
    count = lax.axis_size(axis)
    return lax.ppermute(value, axis, [(i, (i + step) % count) for i in range(count)])


def summed_shares(left, right, axis):
    left_far = turned(left[2], axis, 1)
    right_far = turned(right[2], axis, -1)
    left_back = turned(left[3], axis, -1)
    right_on = turned(right[1], axis, 1)
    left_on = turned(added(left[1], left_far), axis, 1)
    right_back = turned(added(right[3], right_far), axis, -1)
    return total(left[0], left_on, left_back, right[0], right_on, right_back)


def on_device(
    query_vectors, key_vectors, value_vectors, query_gain, level_gain, out_weight, out_grad
):
    heads, rows = query_gain.shape
    dk = query_vectors.shape[1] // heads
    scale = dk ** (-0.5)
    seq_count = lax.axis_size("seq")
    bits = seq_count.bit_length() - 1
    shift_bits = rows.bit_length() - 1
    level_weights = level_weights_of(level_gain)
    gain = query_gain
    chips = seq_count // 2
    groups = [[2 * chip + core for chip in range(chips)] for core in range(2)]
    chip, core = lax.axis_index("seq") // 2, lax.axis_index("seq") % 2
    head = core * (heads // 2) + chip * (heads // 2) // chips
    scan_weights = lax.dynamic_slice(level_weights, (head, shift_bits + 2), (1, bits - 1))
    pair_weights = lax.dynamic_slice(
        level_weights, (core * (heads // 2), shift_bits + 1), (heads // 2, 1)
    )
    index = jnp.stack([lax.axis_index("head"), core])
    core = core.reshape(1)

    key_mine, key_sent = key_state(core, key_vectors, value_vectors, heads)
    key_other = from_sibling(key_sent, "seq")
    key_pieces = swapped(chip_sum(key_mine, key_other, chips), "seq", groups)
    dmix, query_mine, query_sent = mix_grad(core, out_grad, out_weight, query_vectors, gain, heads)
    query_other = from_sibling(query_sent, "seq")
    past_pieces = scan_past(key_pieces, query_mine, query_other, scan_weights)
    joined = swapped(past_pieces, "seq", groups)
    mix, near_queries, near_keys, near_values = near_terms(
        query_vectors, key_vectors, value_vectors, dmix, gain, level_weights, scale, heads
    )
    past_own, past_sent = parts_of(core, pair_weights, joined, key_mine, key_other, True)
    past_came = from_sibling(past_sent, "seq")
    left, right = shares_of(
        index, query_vectors, past_own, past_came, mix, gain, out_weight, scale, heads,
        lax.axis_size("head"),
    )
    layer_out = summed_shares(left, right, "head")
    grad_queries = far_past(core, dmix, gain, past_own, past_came, near_queries, scale, heads)
    future_pieces = scan_future(joined, scan_weights)
    future = swapped(future_pieces, "seq", groups)
    future_own, future_sent = parts_of(core, pair_weights, future, query_mine, query_other, False)
    future_came = from_sibling(future_sent, "seq")
    grad_keys, grad_values = far_future(
        core, key_vectors, value_vectors, future_own, future_came, near_keys, near_values,
        scale, heads,
    )
    return (layer_out, grad_queries, grad_keys, grad_values)


def solution(mesh):
    return jax.shard_map(
        on_device,
        mesh=mesh,
        in_specs=(
            P("seq", "head"),
            P("seq", "head"),
            P("seq", "head"),
            P("head", "seq"),
            P("head", None),
            P("head", None),
            P("seq", None),
        ),
        out_specs=(P(("seq", "head"), None), P("seq", "head"), P("seq", "head"), P("seq", "head")),
        check_vma=False,
    )
```
